128 devices in a mesh: seq: 32 (over z, y, core), exp: 4 (over x).
Axes of the slice: x: 4, y: 4, z: 4, core: 2. Of those that a mesh axis runs over, the one named last changes fastest.
Arguments:
- residual_in: bfloat16 [16384, 2048], P(('seq', 'exp')), may hold values from -6 to 6
- query_input: bfloat16 [16384, 1024], P(('seq', 'exp')), may hold values from -6 to 6
- key_input: bfloat16 [16384, 1024], P(('seq', 'exp')), may hold values from -6 to 6
- value_input: bfloat16 [16384, 2048], P(('seq', 'exp')), may hold values from -6 to 6
- out_gate: bfloat16 [16384, 2048], P(('seq', 'exp')), may hold values from -6 to 6
- write_strength: float32 [16384, 16], P(('seq', 'exp')), may hold values from 0 to 2
- decay_rate: float32 [16384, 16], P(('seq', 'exp')), may hold values from 0 to 1
- head_gain: float32 [128], replicated, may hold values from 0.1 to 1.9
- out_proj: bfloat16 [2048, 2048], P(None, 'exp'), may hold values from -0.125 to 0.125
- post_gain: float32 [2048], replicated, may hold values from 0.1 to 1.9
- expert_ids: int32 [16384, 10], P(('seq', 'exp')), may hold values from 0 to 255, all different within a row; in each aligned block of 128 rows (0 to 127, 128 to 255, ...) at most 8 rows name the same one
- gate_weights: float32 [16384, 10], P(('seq', 'exp')), may hold values from 0.05 to 0.3
- expert_gate: bfloat16 [256, 2048, 512], P(('seq', 'exp')), may hold values from -0.125 to 0.125
- expert_up: bfloat16 [256, 2048, 512], P(('seq', 'exp')), may hold values from -0.125 to 0.125
- expert_down: bfloat16 [256, 512, 2048], P(('seq', 'exp')), may hold values from -0.25 to 0.25
Outputs:
- layer_out: bfloat16 [16384, 2048], P(('seq', 'exp'))
The draws below stay inside these ranges and needn't reach their ends.
Inputs may be any that keep to these rules, and one draw needn't show every extreme that they name: `expert_ids`: each row names 10 different experts. Within the rows of one device (aligned blocks of 128 rows) no expert is named more than 8 times, and in every draw some expert is named exactly 8 times within one device's rows.
All inputs are finite; a program needn't handle non-finite values.
Results may differ from the reference program's by a relative error of at most 0.011.
Values may be sent and summed in bfloat16 or wider, within the bound.
A program may use at most 256 MiB of HBM per device.

```python
import math
from functools import partial
import jax
import jax.numpy as jnp
import numpy as np
from jax import lax

D = 2048
HK = 8
GROUP_VALUE_HEADS = 16
DK = 128
DV = 128
CH = 64
FFE = 512
TOP = 10
EXP_DEV = 2
TOK_DEV = 128
SEQUENCE_TOKENS = 16384
EXPERTS = 256
CAP = 8


def slow_heads(key):
    order_key, count_key = jax.random.split(jax.random.fold_in(key, 101))
    order = jax.random.permutation(order_key, GROUP_VALUE_HEADS)
    count = jax.random.randint(count_key, (), GROUP_VALUE_HEADS // 2, 3 * GROUP_VALUE_HEADS // 4 + 1)
    return order < count


def draw_decay_rate(key, part):
    slow = slow_heads(key)
    every_key = jax.random.split(jax.random.fold_in(key, 303), 6)
    slow_rate = jnp.exp(jax.random.uniform(every_key[0], (GROUP_VALUE_HEADS,), minval=math.log(0.03), maxval=math.log(0.3))) / SEQUENCE_TOKENS
    fast_rate = jnp.exp(jax.random.uniform(every_key[1], (GROUP_VALUE_HEADS,), minval=math.log(1.0 / 50.0), maxval=math.log(1.0 / 30.0)))
    starting_point = jnp.where(slow, slow_rate, fast_rate)
    device_multiplier = jnp.exp(jax.random.uniform(every_key[2], (SEQUENCE_TOKENS // TOK_DEV, GROUP_VALUE_HEADS), minval=math.log(0.5), maxval=math.log(2.0)))
    device_multiplier = jnp.repeat(device_multiplier, TOK_DEV, axis=0)
    coarse_guess = jnp.exp(jax.random.uniform(every_key[3], (SEQUENCE_TOKENS, GROUP_VALUE_HEADS), minval=math.log(0.5), maxval=math.log(2.0)))
    spots = jax.random.randint(every_key[4], (3,), 0, SEQUENCE_TOKENS)
    removed_part = jnp.any(jnp.arange(SEQUENCE_TOKENS)[:, None] == spots[None, :], axis=1)
    sudden_jump = jax.random.uniform(every_key[5], (SEQUENCE_TOKENS, GROUP_VALUE_HEADS), minval=0.22, maxval=0.4)
    return starting_point[None, :] * device_multiplier * coarse_guess + jnp.where(removed_part[:, None], sudden_jump, 0.0)


def draw_write_strength(key, part):
    slow = slow_heads(key)
    small_key, large_key = jax.random.split(jax.random.fold_in(key, 202))
    small = jnp.exp(jax.random.uniform(small_key, (SEQUENCE_TOKENS, GROUP_VALUE_HEADS), minval=math.log(0.25), maxval=math.log(1.0)))
    large = jax.random.uniform(large_key, (SEQUENCE_TOKENS, GROUP_VALUE_HEADS), minval=0.2, maxval=0.9)
    return jnp.where(slow[None, :], 2.0 - small * DK / SEQUENCE_TOKENS, large)


def block_levels(stream_key, dims, shards, smallest, top_value):
    def one(position, blocks):
        steps = jax.random.uniform(jax.random.fold_in(jax.random.fold_in(stream_key, 6), position), (blocks,), jnp.float32, smallest / len(shards), top_value / len(shards))
        return jnp.repeat(jnp.exp(steps), dims[position] // blocks).reshape((-1,) + (1,) * (len(dims) - position - 1))

    factor_of = one(*shards[0])
    for cut in shards[1:]:
        factor_of = factor_of * one(*cut)
    return factor_of


def deal_out(key, own, number, rows, amount, top, most, skew):
    order = jax.random.permutation(key, amount)
    crowded, usual = shares(amount, rows * top, most, skew, True), shares(amount, rows * top, most, skew, False)
    places = jnp.arange(amount)

    def named(lengths, turn):
        used = int((lengths > 0).sum())
        fixed = max(1, used // 4)
        shifted = fixed + (places - fixed + turn * (used - fixed)) % max(1, amount - fixed)
        return jnp.zeros((amount,), jnp.int32).at[order[jnp.where(places < fixed, places, shifted)]].set(jnp.asarray(lengths, jnp.int32))

    lengths = jnp.where(number % 4 == 0, named(crowded, number // 4), named(usual, number - number // 4 - 1))
    mixed = jax.random.permutation(jax.random.fold_in(own, 3), amount)
    donor, receiver = mixed[0:amount // 2 * 2:2], mixed[1:amount // 2 * 2:2]
    margin = jnp.minimum(lengths[donor] - 1, most - lengths[receiver]) // 2
    margin = jnp.where((donor == order[0]) | (receiver == order[0]) | (lengths[receiver] == 0), 0, jnp.maximum(margin, 0))
    shifted = jax.random.randint(jax.random.fold_in(own, 4), (amount // 2,), 0, 1 << 20) % (margin + 1)
    lengths = lengths.at[donor].add(-shifted).at[receiver].add(shifted)
    members = jnp.searchsorted(jnp.cumsum(lengths), jnp.arange(rows * top), side="right").astype(jnp.int32)
    table = members.reshape(top, rows).T
    table = table[jax.random.permutation(jax.random.fold_in(own, 1), rows)]
    turn = jax.random.randint(jax.random.fold_in(own, 2), (rows, 1), 0, top)
    return jnp.take_along_axis(table, (jnp.arange(top)[None, :] + turn) % top, axis=1)


def shares(amount, total, limit, slope, full):
    weights = [(1 << 20) // math.isqrt(grade ** slope) + 1 for grade in range(1, amount + 1)]
    largest = limit if full else min(limit, max(-(-total // amount), total * weights[0] // sum(weights)))
    least = 1 if total - largest >= amount - 1 else 0
    given, surplus = [largest] + [least] * (amount - 1), total - largest - least * (amount - 1)
    while surplus > 0:
        free = [i for i in range(1, amount) if given[i] < largest] or [i for i in range(1, amount) if given[i] < limit]
        mass, left = sum([weights[i] for i in free]), surplus
        for i in free:
            more = min(limit - given[i], max(1, left * weights[i] // mass), surplus)
            given[i] = given[i] + more
            surplus = surplus - more
    return np.array(given)


def bell_draw(key, extent, scale, bound, cuts=(), held_as=jnp.bfloat16):
    factor_of = block_levels(key, extent, cuts, -0.22, 0.18) if cuts else 1.0
    values = jax.random.normal(key, extent, jnp.float32) * scale * factor_of
    return jnp.minimum(jnp.maximum(values, -bound), bound).astype(held_as)


def setup_inputs(seed: int = 0) -> dict:
    keys = jax.random.split(jax.random.key(seed), 16)
    residual_in = bell_draw(keys[0], (SEQUENCE_TOKENS, D), 1.0, 6.0, ((0, 128),))
    query_input = bell_draw(keys[1], (SEQUENCE_TOKENS, HK * DK), 1.0, 6.0, ((0, 128),))
    key_input = bell_draw(keys[2], (SEQUENCE_TOKENS, HK * DK), 1.0, 6.0, ((0, 128),))
    value_input = bell_draw(keys[3], (SEQUENCE_TOKENS, GROUP_VALUE_HEADS * DV), 1.0, 6.0, ((0, 128),))
    out_gate = bell_draw(keys[4], (SEQUENCE_TOKENS, GROUP_VALUE_HEADS * DV), 1.0, 6.0, ((0, 128),))
    write_strength = draw_write_strength(jax.random.fold_in(keys[15], 71), 0)
    decay_rate = draw_decay_rate(jax.random.fold_in(keys[15], 71), 0)
    head_gain = jnp.clip(1.0 + 0.18 * jax.random.normal(keys[7], (DV,), jnp.float32), 0.1, 1.9)
    out_proj = bell_draw(keys[8], (GROUP_VALUE_HEADS * DV, D), (GROUP_VALUE_HEADS * DV) ** -0.5, 0.125, ((1, 4),))
    post_gain = jnp.clip(1.0 + 0.18 * jax.random.normal(keys[9], (D,), jnp.float32), 0.1, 1.9)
    expert_ids_keys = jax.random.split(jax.random.fold_in(keys[10], 1), SEQUENCE_TOKENS // TOK_DEV)
    expert_ids_turns = jax.random.permutation(jax.random.fold_in(keys[10], 3), SEQUENCE_TOKENS // TOK_DEV)
    expert_ids = jax.vmap(lambda own, number: deal_out(jax.random.fold_in(keys[10], 2), own, number, TOK_DEV, EXPERTS, TOP, CAP, 2))(expert_ids_keys, expert_ids_turns).reshape((SEQUENCE_TOKENS, TOP))
    gate_weights = jnp.clip(0.05 + 0.25 * jax.random.uniform(keys[11], (SEQUENCE_TOKENS, TOP), jnp.float32) ** block_levels(keys[11], (SEQUENCE_TOKENS, TOP), ((0, 128),), -0.2, 0.2), 0.05, 0.3)
    expert_gate = bell_draw(keys[12], (EXPERTS, D, FFE), D ** -0.5, 0.125, ((0, 128),))
    expert_up = bell_draw(keys[13], (EXPERTS, D, FFE), D ** -0.5, 0.125, ((0, 128),))
    expert_down = bell_draw(keys[14], (EXPERTS, FFE, D), FFE ** -0.5, 0.25, ((0, 128),))
    return {"residual_in": residual_in, "query_input": query_input, "key_input": key_input, "value_input": value_input, "out_gate": out_gate, "write_strength": write_strength, "decay_rate": decay_rate, "head_gain": head_gain, "out_proj": out_proj, "post_gain": post_gain, "expert_ids": expert_ids, "gate_weights": gate_weights, "expert_gate": expert_gate, "expert_up": expert_up, "expert_down": expert_down}


largest_value = lax.Precision.HIGHEST

def unit_rows(block):
    return block * lax.rsqrt(lax.optimization_barrier(jnp.sum(block * block, axis=-1, keepdims=True)) + 1e-06)

def block_terms(query_block, key_block, value_block, strength, rate):
    block_len = key_block.shape[1]
    width = key_block.shape[2]
    logs = jnp.cumsum(-rate, axis=1)
    log_gap = logs[:, :, None] - logs[:, None, :]
    row_ids = jnp.arange(block_len)[:, None]
    column_ids = jnp.arange(block_len)[None, :]
    inclusive = (row_ids >= column_ids)[None]
    strict = (row_ids > column_ids)[None]
    ratio = jnp.where(inclusive, jnp.exp(jnp.where(inclusive, log_gap, 0.0)), 0.0)
    key_gram = jnp.einsum('htd,hsd->hts', key_block, key_block, precision=largest_value)
    system = jnp.where(strict, ratio * key_gram, 0.0) * strength[:, :, None] + jnp.eye(block_len, dtype=jnp.float32)
    growth = jnp.exp(logs)
    newest_value = jax.scipy.linalg.solve_triangular(system, strength[:, :, None] * value_block, lower=True, unit_diagonal=True)
    key_matrix = jax.scipy.linalg.solve_triangular(system, (strength * growth)[:, :, None] * key_block, lower=True, unit_diagonal=True)
    mixed_query = ratio * jnp.einsum('htd,hsd->hts', query_block, key_block, precision=largest_value)
    faded_key = key_block * jnp.exp(logs[:, -1:] - logs)[:, :, None]
    transition_matrix = growth[:, -1][:, None, None] * jnp.eye(width, dtype=jnp.float32) - jnp.einsum('hck,hcj->hkj', faded_key, key_matrix, precision=largest_value)
    increment_term = jnp.einsum('btx,btw->bxw', faded_key, newest_value, precision=largest_value)
    return (query_block * growth[:, :, None], mixed_query, newest_value, key_matrix, transition_matrix, increment_term)

def block_output(passed_state, rescaled_query, mixed_query, newest_value, key_matrix):
    state_update = newest_value - jnp.einsum('lxw,lwp->lxp', key_matrix, passed_state, precision=largest_value)
    return jnp.einsum('lxw,lwp->lxp', rescaled_query, passed_state, precision=largest_value) + jnp.einsum('xib,xbp->xip', mixed_query, state_update, precision=largest_value)

def prepare(query_input, key_input, value_input, write_strength, decay_rate):
    tok_rows = key_input.shape[0]
    blocks_here = tok_rows // CH
    head_group = GROUP_VALUE_HEADS // HK
    query_unit = unit_rows(query_input.reshape(tok_rows, HK, DK).astype(jnp.float32)) * DK ** (-0.5)
    key_unit = unit_rows(key_input.reshape(tok_rows, HK, DK).astype(jnp.float32))
    query_unit = jnp.repeat(query_unit, head_group, axis=1)
    key_unit = jnp.repeat(key_unit, head_group, axis=1)
    value_heads = value_input.reshape(tok_rows, GROUP_VALUE_HEADS, DV).astype(jnp.float32)

    def blocked(array):
        shaped = array.reshape((blocks_here, CH) + array.shape[1:])
        return jnp.swapaxes(shaped, 1, 2)
    return jax.vmap(block_terms)(blocked(query_unit), blocked(key_unit), blocked(value_heads), blocked(write_strength), blocked(decay_rate))

def finish_core(outputs, out_gate, head_gain):
    tok_rows = out_gate.shape[0]
    recurrent = jnp.swapaxes(outputs, 1, 2).reshape(tok_rows, GROUP_VALUE_HEADS, DV)
    inv_rms = lax.rsqrt(lax.optimization_barrier(jnp.mean(recurrent * recurrent, axis=2, keepdims=True)) + 1e-06)
    gate_act = jax.nn.silu(out_gate.reshape(tok_rows, GROUP_VALUE_HEADS, DV).astype(jnp.float32))
    return (recurrent * inv_rms * head_gain * gate_act).astype(jnp.bfloat16).reshape(tok_rows, GROUP_VALUE_HEADS * DV)

def post_norm(hidden_state, post_gain):
    widened = hidden_state.astype(jnp.float32)
    return (widened * lax.rsqrt(lax.optimization_barrier(jnp.mean(widened * widened, axis=1, keepdims=True)) + 1e-06) * post_gain).astype(jnp.bfloat16)

def slot_index(expert_ids, experts, capacity):
    flat_ids = expert_ids.reshape(-1)
    onehot = (flat_ids[:, None] == jnp.arange(experts, dtype=jnp.int32)[None, :]).astype(jnp.int32)
    before = jnp.cumsum(onehot, axis=0) - onehot
    return (flat_ids * capacity + lax.optimization_barrier(jnp.sum(before * onehot, axis=1))).astype(jnp.int32)

def expert_rows(block, weight_gate, weight_up, weight_down):
    gate_part = jnp.dot(block.astype(jnp.float32), weight_gate.astype(jnp.float32), preferred_element_type=jnp.float32)
    up_part = jnp.dot(block.astype(jnp.float32), weight_up.astype(jnp.float32), preferred_element_type=jnp.float32)
    inner = (jax.nn.silu(gate_part) * up_part).astype(jnp.bfloat16)
    return jnp.dot(inner.astype(jnp.float32), weight_down.astype(jnp.float32), preferred_element_type=jnp.float32).astype(jnp.bfloat16)

def reference(residual_in, query_input, key_input, value_input, out_gate, write_strength, decay_rate, head_gain, out_proj, post_gain, expert_ids, gate_weights, expert_gate, expert_up, expert_down):
    tok_rows = residual_in.shape[0]
    pieces = prepare(query_input, key_input, value_input, write_strength, decay_rate)

    def emit_block(passed_state, item):
        rescaled_query, mixed_query, newest_value, key_matrix, transition_matrix, increment_term = item
        emitted = block_output(passed_state, rescaled_query, mixed_query, newest_value, key_matrix)
        moved_forward = jnp.einsum('aip,ape->aie', transition_matrix, passed_state, precision=largest_value) + increment_term
        return (moved_forward, emitted)
    _, outputs = lax.scan(emit_block, jnp.zeros((GROUP_VALUE_HEADS, DK, DV), jnp.float32), pieces)
    core_out = finish_core(outputs, out_gate, head_gain)
    mixer_out = jnp.dot(core_out.astype(jnp.float32), out_proj.astype(jnp.float32), preferred_element_type=jnp.float32)
    hidden_state = (residual_in.astype(jnp.float32) + mixer_out).astype(jnp.bfloat16)
    normed = post_norm(hidden_state, post_gain)
    devices = EXPERTS // EXP_DEV
    per_device = expert_ids.reshape(devices, TOK_DEV * TOP)
    local_slots = lax.map(partial(slot_index, experts=EXPERTS, capacity=CAP), per_device)
    owner = jnp.arange(devices, dtype=jnp.int32)[:, None]
    global_slots = (local_slots // CAP * (devices * CAP) + owner * CAP + local_slots % CAP).astype(jnp.int32)
    token_ids = (jnp.arange(tok_rows * TOP, dtype=jnp.int32) // TOP).astype(jnp.int32)
    source = jnp.full((EXPERTS * devices * CAP,), tok_rows, dtype=jnp.int32).at[global_slots.reshape(-1)].set(token_ids)
    padded = jnp.concatenate([normed, jnp.zeros((1, D), jnp.bfloat16)], axis=0)

    def serve(item):
        table, weight_gate, weight_up, weight_down = item
        return expert_rows(padded[table], weight_gate, weight_up, weight_down)
    results = lax.map(serve, (source.reshape(EXPERTS, devices * CAP), expert_gate, expert_up, expert_down)).reshape(-1, D)

    def combine(item):
        slots, weights = item
        picked = results[slots].reshape(TOK_DEV, TOP, D).astype(jnp.float32)
        return lax.optimization_barrier(jnp.sum(weights[:, :, None] * picked, axis=1))
    routed = lax.map(combine, (global_slots, gate_weights.reshape(devices, TOK_DEV, TOP))).reshape(tok_rows, D)
    return (hidden_state.astype(jnp.float32) + routed).astype(jnp.bfloat16)
```

```python
from functools import partial

import jax
import jax.numpy as jnp
from jax import lax
from jax.experimental import pallas as pl
from jax.experimental.pallas import tpu as pltpu
from jax.sharding import PartitionSpec as P

D = 2048
HK = 8
HV = 16
DK = 128
DV = 128
TOP = 10
GROUP = 16

F32 = jnp.float32
BF16 = jnp.bfloat16
MESH = pl.DeviceIdType.MESH


def mm(a, b):
    return jnp.dot(a, b, preferred_element_type=F32)


def mm_t(a, b):
    return lax.dot_general(a, b, (((1,), (1,)), ((), ())), preferred_element_type=F32)


def split(x):
    high = x.astype(BF16)
    return high, (x - high.astype(F32)).astype(BF16)


def mm3(a, b):
    return mm(a[0], b[0]) + (mm(a[0], b[1]) + mm(a[1], b[0]))


def iota(axis):
    return lax.broadcasted_iota(jnp.int32, (128, 128), axis)


def rows_of(row):
    return jnp.broadcast_to(row, (128, 128))


def unit_inverse(lower):
    row, col = iota(0), iota(1)
    eye = jnp.where(row == col, 1.0, 0.0)
    inverse = eye - jnp.where((row >> 1) == (col >> 1), lower, 0.0)
    for level in range(1, 7):
        mask = ((row >> (level + 1)) == (col >> (level + 1))) & ((row >> level) != (col >> level))
        part = split(jnp.where(mask, lower, 0.0))
        blocks = split(inverse)
        inverse = inverse - mm3(blocks, split(mm3(part, blocks)))
    return inverse


def mixer_kernel(
    seq_size,
    exp_size,
    q_ref,
    k_ref,
    v_ref,
    gate_ref,
    rate_ref,
    beta_ref,
    gain_ref,
    out_ref,
    logs,
    local_out,
    query_high,
    query_low,
    maps,
    maps_in,
    prefix,
    groups_in,
    states,
    states_in,
    send1,
    recv1,
    send2,
    recv2,
    send3,
    recv3,
):
    lines = GROUP // exp_size
    groups = seq_size // lines
    seq, exp = lax.axis_index("seq"), lax.axis_index("exp")
    group = seq // lines
    rank = (seq % lines) * exp_size + exp

    def device(of_group, of_rank):
        return (of_group * lines + of_rank // exp_size, of_rank % exp_size)

    barrier = pltpu.get_barrier_semaphore()

    def greet_rank(step, carry):
        pl.semaphore_signal(barrier, inc=1, device_id=device(group, lax.rem(rank + step, GROUP)), device_id_type=MESH)
        return carry

    def greet_group(step, carry):
        pl.semaphore_signal(barrier, inc=1, device_id=device(lax.rem(group + step, groups), rank), device_id_type=MESH)
        return carry

    lax.fori_loop(1, GROUP, greet_rank, 0)
    lax.fori_loop(1, groups, greet_group, 0)
    pl.semaphore_wait(barrier, GROUP - 1 + groups - 1)

    row, col = iota(0), iota(1)
    upto = jnp.where(row <= col, 1.0, 0.0).astype(BF16)
    rate = rate_ref[...]
    first, rest = split(rate)
    last = (rate - first.astype(F32) - rest.astype(F32)).astype(BF16)
    logs[...] = -(mm(first, upto) + (mm(rest, upto) + mm(last, upto)))

    def map_copy(head, to):
        return pltpu.make_async_remote_copy(
            src_ref=maps.at[head],
            dst_ref=maps_in.at[to],
            send_sem=send1.at[head],
            recv_sem=recv1.at[to],
            device_id=device(group, head),
            device_id_type=MESH,
        )

    def map_keep(head, to):
        return pltpu.make_async_copy(maps.at[head], maps_in.at[to], recv1.at[to])

    def key_head(kh, carry):
        columns = pl.ds(pl.multiple_of(kh * DK, DK), DK)
        k_raw, q_raw = k_ref[:, columns], q_ref[:, columns]
        k_wide, q_wide = k_raw.astype(F32), q_raw.astype(F32)
        k_inv = lax.rsqrt(jnp.sum(k_wide * k_wide, axis=1, keepdims=True) + 1e-6)
        q_inv = lax.rsqrt(jnp.sum(q_wide * q_wide, axis=1, keepdims=True) + 1e-6) * DK ** (-0.5)
        k_inv = jnp.broadcast_to(k_inv, (128, 128))
        k_inv_row = k_inv.T
        k_t = k_wide.T.astype(BF16)
        gram = mm_t(k_raw, k_raw) * k_inv * k_inv_row
        mixed = mm_t(q_raw, k_raw) * q_inv * k_inv_row
        for part in range(HV // HK):
            h = kh * (HV // HK) + part
            head_columns = pl.ds(pl.multiple_of(h * DV, DV), DV)
            log_row = rows_of(logs[pl.ds(h, 1), :])
            log_col = log_row.T
            beta_row = rows_of(beta_ref[pl.ds(h, 1), :])
            beta_col = beta_row.T
            ratio = jnp.where(row >= col, jnp.exp(jnp.where(row >= col, log_col - log_row, 0.0)), 0.0)
            inverse = unit_inverse(jnp.where(row > col, ratio * gram, 0.0) * beta_col)
            v_raw = v_ref[:, head_columns]
            weights = split(inverse * beta_row)
            newest = mm(weights[0], v_raw) + mm(weights[1], v_raw)
            weights = split(inverse * (beta_row * jnp.exp(log_row) * k_inv_row))
            key_matrix = mm(weights[0], k_raw) + mm(weights[1], k_raw)
            log_last = jnp.broadcast_to(logs[pl.ds(h, 1), 127:128], (128, 128))
            fade = k_inv * jnp.exp(log_last - log_col)
            side = split(key_matrix * fade)
            moved = mm(k_t, side[0]) + mm(k_t, side[1])
            maps[h, :, :DK] = jnp.where(row == col, jnp.exp(log_last), 0.0) - moved
            side = split(newest * fade)
            maps[h, :, DK:] = mm(k_t, side[0]) + mm(k_t, side[1])

            @pl.when(h != rank)
            def _():
                map_copy(h, rank).start()

            @pl.when(h == rank)
            def _():
                map_keep(h, rank).start()

            mix = split(mixed * ratio)
            local_out[h] = mm3(mix, split(newest))
            effective = split(q_wide * q_inv * jnp.exp(log_col) - mm3(mix, split(key_matrix)))
            query_high[h] = effective[0]
            query_low[h] = effective[1]
        return carry

    lax.fori_loop(0, HK, key_head, 0)

    map_keep(0, 0).wait()
    prefix[0] = maps_in[0]

    def chain(index, carry):
        map_keep(index, index).wait()
        step = split(maps_in[index, :, :DK])
        before = prefix[index - 1]
        prefix[index, :, :DK] = mm3(step, split(before[:, :DK]))
        prefix[index, :, DK:] = mm3(step, split(before[:, DK:])) + maps_in[index, :, DK:]
        return carry

    lax.fori_loop(1, GROUP, chain, 0)

    def group_copy(to, source):
        return pltpu.make_async_remote_copy(
            src_ref=prefix.at[GROUP - 1],
            dst_ref=groups_in.at[source],
            send_sem=send2.at[to],
            recv_sem=recv2.at[source],
            device_id=device(to, rank),
            device_id_type=MESH,
        )

    def send_group(to, carry):
        group_copy(to, group).start()
        return carry

    lax.fori_loop(group + 1, groups, send_group, 0)

    def enter(source, state):
        group_copy(group, source).wait_recv()
        return mm3(split(groups_in[source, :, :DK]), split(state)) + groups_in[source, :, DK:]

    entering = split(lax.fori_loop(0, group, enter, jnp.zeros((DK, DV), F32)))

    def state_copy(to, head):
        return pltpu.make_async_remote_copy(
            src_ref=states.at[to],
            dst_ref=states_in.at[head],
            send_sem=send3.at[to],
            recv_sem=recv3.at[head],
            device_id=device(group, to),
            device_id_type=MESH,
        )

    def state_keep(to, head):
        return pltpu.make_async_copy(states.at[to], states_in.at[head], recv3.at[head])

    def give(to):
        @pl.when(to != rank)
        def _():
            state_copy(to, rank).start()

        @pl.when(to == rank)
        def _():
            state_keep(to, rank).start()

    states[0] = entering[0]
    give(0)

    def spread(index, carry):
        moved = mm3(split(prefix[index - 1, :, :DK]), entering) + prefix[index - 1, :, DK:]
        states[index] = moved.astype(BF16)
        give(index)
        return carry

    lax.fori_loop(1, GROUP, spread, 0)

    gain = gain_ref[...]

    def finish(h, carry):
        columns = pl.ds(pl.multiple_of(h * DV, DV), DV)
        gate = gate_ref[:, columns].astype(F32)
        scale = gain * (gate / (1.0 + jnp.exp(-gate)))
        state_keep(h, h).wait()
        state = states_in[h]
        out = local_out[h] + (mm(query_high[h], state) + mm(query_low[h], state))
        inv_rms = lax.rsqrt(jnp.sum(out * out, axis=1, keepdims=True) * (1.0 / DV) + 1e-6)
        out_ref[:, columns] = (out * inv_rms * scale).astype(BF16)
        return carry

    lax.fori_loop(0, HV, finish, 0)

    def drain(index, carry):
        @pl.when(index != rank)
        def _():
            map_copy(index, rank).wait_send()
            state_copy(index, rank).wait_send()

        return carry

    lax.fori_loop(0, GROUP, drain, 0)

    def drain_group(to, carry):
        group_copy(to, group).wait_send()
        return carry

    lax.fori_loop(group + 1, groups, drain_group, 0)


def mixer_core(query, key, value, gate, strength, rate, head_gain):
    seq_size, exp_size = lax.axis_size("seq"), lax.axis_size("exp")
    groups = seq_size * exp_size // GROUP
    tokens = query.shape[0]
    vmem = pl.BlockSpec(memory_space=pltpu.VMEM)
    return pl.pallas_call(
        partial(mixer_kernel, seq_size, exp_size),
        out_shape=jax.ShapeDtypeStruct((tokens, HV * DV), BF16),
        in_specs=[vmem] * 7,
        out_specs=vmem,
        scratch_shapes=[
            pltpu.VMEM((HV, tokens), F32),
            pltpu.VMEM((HV, tokens, DV), F32),
            pltpu.VMEM((HV, tokens, DK), BF16),
            pltpu.VMEM((HV, tokens, DK), BF16),
            pltpu.VMEM((HV, DK, DK + DV), F32),
            pltpu.VMEM((GROUP, DK, DK + DV), F32),
            pltpu.VMEM((GROUP, DK, DK + DV), F32),
            pltpu.VMEM((groups, DK, DK + DV), F32),
            pltpu.VMEM((GROUP, DK, DV), BF16),
            pltpu.VMEM((HV, DK, DV), BF16),
            pltpu.SemaphoreType.DMA((HV,)),
            pltpu.SemaphoreType.DMA((GROUP,)),
            pltpu.SemaphoreType.DMA((groups,)),
            pltpu.SemaphoreType.DMA((groups,)),
            pltpu.SemaphoreType.DMA((GROUP,)),
            pltpu.SemaphoreType.DMA((HV,)),
        ],
        compiler_params=pltpu.CompilerParams(
            collective_id=0, has_side_effects=True, vmem_limit_bytes=32 * 1024 * 1024
        ),
        cost_estimate=pl.CostEstimate(flops=8_000_000_000, bytes_accessed=4_000_000, transcendentals=0),
    )(query, key, value, gate, rate.T, strength.T, head_gain.reshape(1, DV))


def post_norm(hidden_state, post_gain):
    widened = hidden_state.astype(F32)
    return (widened * lax.rsqrt(jnp.mean(widened * widened, axis=1, keepdims=True) + 1e-6) * post_gain).astype(BF16)


def slot_tables(expert_ids, gate_weights, experts, capacity):
    tokens = expert_ids.shape[0]
    named = expert_ids.T[:, None, :] == jnp.arange(experts, dtype=jnp.int32)[None, :, None]
    weight = jnp.sum(jnp.where(named, gate_weights.T[:, None, :], 0.0), axis=0)
    chosen = jnp.any(named, axis=0)
    earlier = jnp.arange(tokens)[:, None] < jnp.arange(tokens)[None, :]
    before = jnp.dot(chosen.astype(BF16), earlier.astype(BF16), preferred_element_type=F32).astype(jnp.int32)
    before = jnp.where(chosen, before, -1)
    here = before[:, None, :] == jnp.arange(capacity, dtype=jnp.int32)[None, :, None]
    pick = here.astype(BF16).reshape(experts * capacity, tokens)
    mix = jnp.where(here, weight[:, None, :], 0.0).reshape(experts * capacity, tokens)
    return pick, mix


def shards(
    residual_in,
    query_input,
    key_input,
    value_input,
    out_gate,
    write_strength,
    decay_rate,
    head_gain,
    out_proj,
    post_gain,
    expert_ids,
    gate_weights,
    expert_gate,
    expert_up,
    expert_down,
):
    tokens = residual_in.shape[0]
    devices = lax.axis_size(("seq", "exp"))
    local_experts = expert_gate.shape[0]
    experts = local_experts * devices
    capacity = max(2, tokens * TOP * 8 // (5 * experts))
    all_proj = lax.all_gather(out_proj, "exp", axis=1, tiled=True)
    pick, mix = slot_tables(expert_ids, gate_weights, experts, capacity)
    core_out = mixer_core(query_input, key_input, value_input, out_gate, write_strength, decay_rate, head_gain)
    mixer_out = jnp.dot(core_out, all_proj, preferred_element_type=F32)
    hidden_state = (residual_in.astype(F32) + mixer_out).astype(BF16)
    normed = post_norm(hidden_state, post_gain)
    send = jnp.dot(pick, normed, preferred_element_type=F32).astype(BF16)
    send = send.reshape(devices, local_experts * capacity, D)
    received = lax.all_to_all(send, ("seq", "exp"), split_axis=0, concat_axis=0, tiled=True)
    received = received.reshape(devices, local_experts, capacity, D)
    results = []
    for e in range(local_experts):
        block = received[:, e].reshape(devices * capacity, D)
        gate_part = jnp.dot(block, expert_gate[e], preferred_element_type=F32)
        up_part = jnp.dot(block, expert_up[e], preferred_element_type=F32)
        inner = (gate_part / (1.0 + jnp.exp(-gate_part)) * up_part).astype(BF16)
        result = jnp.dot(inner, expert_down[e], preferred_element_type=F32).astype(BF16)
        results.append(result.reshape(devices, 1, capacity, D))
    result = jnp.concatenate(results, axis=1).reshape(devices, local_experts * capacity, D)
    returned = lax.all_to_all(result, ("seq", "exp"), split_axis=0, concat_axis=0, tiled=True)
    returned = returned.reshape(experts * capacity, D)
    mix_high = mix.astype(BF16)
    mix_low = (mix - mix_high.astype(F32)).astype(BF16)
    both = lax.dot_general(
        jnp.concatenate([mix_high, mix_low], axis=1),
        returned,
        (((0,), (0,)), ((), ())),
        preferred_element_type=F32,
    )
    routed = both[:tokens] + both[tokens:]
    return (hidden_state.astype(F32) + routed).astype(BF16)


def solution(mesh):
    both = ("seq", "exp")
    placed = (
        P(both, None),
        P(both, None),
        P(both, None),
        P(both, None),
        P(both, None),
        P(both, None),
        P(both, None),
        P(),
        P(None, "exp"),
        P(),
        P(both, None),
        P(both, None),
        P(both, None, None),
        P(both, None, None),
        P(both, None, None),
    )
    return jax.shard_map(shards, mesh=mesh, in_specs=placed, out_specs=P(both, None), check_vma=False)
```

```python
from functools import partial

import jax
import jax.numpy as jnp
from jax import lax
from jax.experimental import pallas as pl
from jax.experimental.pallas import tpu as pltpu
from jax.sharding import PartitionSpec as P

D = 2048
HK = 8
HV = 16
DK = 128
DV = 128
TOP = 10
TOGETHER = 1
GROUP = 16

F32 = jnp.float32
BF16 = jnp.bfloat16
MESH = pl.DeviceIdType.MESH


def mm(a, b):
    return jnp.dot(a, b, preferred_element_type=F32)


def mm_t(a, b):
    return lax.dot_general(a, b, (((1,), (1,)), ((), ())), preferred_element_type=F32)


def split(x):
    high = x.astype(BF16)
    return high, (x - high.astype(F32)).astype(BF16)


def mm3(a, b):
    return mm(a[0], b[0]) + (mm(a[0], b[1]) + mm(a[1], b[0]))


def iota(axis):
    return lax.broadcasted_iota(jnp.int32, (128, 128), axis)


def rows_of(row):
    return jnp.broadcast_to(row, (128, 128))


def unit_inverse(lower):
    row, col = iota(0), iota(1)
    eye = jnp.where(row == col, 1.0, 0.0)
    inverse = eye - jnp.where((row >> 1) == (col >> 1), lower, 0.0)
    for level in range(1, 7):
        mask = ((row >> (level + 1)) == (col >> (level + 1))) & ((row >> level) != (col >> level))
        part = split(jnp.where(mask, lower, 0.0))
        blocks = split(inverse)
        inverse = inverse - mm3(blocks, split(mm3(part, blocks)))
    return inverse


def mixer_kernel(
    seq_size,
    exp_size,
    stride,
    q_hbm,
    k_hbm,
    v_hbm,
    gate_hbm,
    residual_hbm,
    proj_hbm,
    rate_ref,
    beta_ref,
    gain_ref,
    post_gain_ref,
    hidden_ref,
    normed_ref,
    q_ref,
    k_ref,
    v_ref,
    gate_ref,
    residual_ref,
    proj,
    core_out,
    logs,
    local_out,
    query_high,
    query_low,
    maps,
    adds,
    maps_in,
    adds_in,
    prefix,
    prefix_add,
    last_add,
    groups_in,
    groups_add,
    states,
    states_in,
    load,
    send1,
    recv1,
    send2,
    recv2,
    send3,
    recv3,
    proj_send,
    proj_recv,
):
    lines = GROUP // exp_size
    groups = seq_size // lines
    seq, exp = lax.axis_index("seq"), lax.axis_index("exp")
    group = seq // lines
    rank = (seq % lines) * exp_size + exp

    loads = [
        pltpu.make_async_copy(source, target, load.at[number])
        for number, (source, target) in enumerate(
            [
                (k_hbm, k_ref),
                (q_hbm, q_ref),
                (v_hbm, v_ref),
                (gate_hbm, gate_ref),
                (residual_hbm, residual_ref),
                (proj_hbm, proj.at[exp]),
            ]
        )
    ]
    for copy in loads:
        copy.start()

    def device(of_group, of_rank):
        return (of_group * lines + of_rank // exp_size, of_rank % exp_size)

    core = seq % 2
    spot = (seq // stride) % 4

    def ring_seq(shift):
        return seq + ((spot + shift) % 4 - spot) * stride

    def ring_exp(shift):
        return lax.rem(exp + shift, 4)

    partner = (seq + 1 - 2 * core, exp)
    rows = proj_hbm.shape[0] // 8
    half = rows // 2

    def piece(x_shift, spot_shift, begin, size):
        row = pl.multiple_of(core * (4 * rows) + (spot + spot_shift) % 4 * rows + begin, half)
        return proj.at[ring_exp(x_shift), pl.ds(row, size)]

    counter = [0]

    def proj_copy(ref, recv_index, to, source=None):
        number = counter[0]
        counter[0] += 1
        return pltpu.make_async_remote_copy(
            src_ref=ref if source is None else source,
            dst_ref=ref,
            send_sem=proj_send.at[number],
            recv_sem=proj_recv.at[recv_index],
            device_id=to,
            device_id_type=MESH,
        )

    def landing(ref, recv_index):
        return pltpu.make_async_copy(ref, ref, proj_recv.at[recv_index])

    own = proj_hbm.at[pl.ds(pl.multiple_of(core * (4 * rows) + spot * rows, half), rows)]
    mine = piece(0, 0, 0, rows)
    right, left = (seq, ring_exp(1)), (seq, ring_exp(3))
    above, below = (ring_seq(1), exp), (ring_seq(3), exp)
    x_first = [proj_copy(mine, 0, right, own), proj_copy(mine, 1, left, own)]
    x_second = [proj_copy(piece(3, 0, 0, half), 2, right), proj_copy(piece(1, 0, half, half), 3, left)]
    x_landing = [
        landing(piece(3, 0, 0, rows), 0),
        landing(piece(1, 0, 0, rows), 1),
        landing(piece(2, 0, 0, half), 2),
        landing(piece(2, 0, half, half), 3),
    ]
    shifts = (3, 1, 2)
    z_first, z_second, z_landing, across, across_landing = [], [], [], [], []
    for number, shift in enumerate(shifts):
        at = 4 + 4 * number
        z_first.append(
            [proj_copy(piece(shift, 0, 0, rows), at, above), proj_copy(piece(shift, 0, 0, rows), at + 1, below)]
        )
        z_second.append(
            [proj_copy(piece(shift, 3, 0, half), at + 2, above), proj_copy(piece(shift, 1, half, half), at + 3, below)]
        )
        z_landing.append(
            [
                landing(piece(shift, 3, 0, rows), at),
                landing(piece(shift, 1, 0, rows), at + 1),
                landing(piece(shift, 2, 0, half), at + 2),
                landing(piece(shift, 2, half, half), at + 3),
            ]
        )
        across.append([proj_copy(piece(shift, n, 0, rows), 16 + 4 * number + n, partner) for n in range(4)])
        other = (1 - core) * (4 * rows)
        across_landing.append(
            [
                landing(
                    proj.at[
                        ring_exp(shift), pl.ds(pl.multiple_of(other + (spot + n) % 4 * rows, half), rows)
                    ],
                    16 + 4 * number + n,
                )
                for n in range(4)
            ]
        )

    barrier = pltpu.get_barrier_semaphore()

    def greet(to):
        pl.semaphore_signal(barrier, inc=1, device_id=to, device_id_type=MESH)

    def greet_rank(step, carry):
        greet(device(group, lax.rem(rank + step, GROUP)))
        return carry

    def greet_group(step, carry):
        greet(device(lax.rem(group + step, groups), rank))
        return carry

    lax.fori_loop(1, GROUP, greet_rank, 0)
    lax.fori_loop(1, groups, greet_group, 0)
    for to in (right, left, above, below, partner):
        greet(to)
    pl.semaphore_wait(barrier, GROUP - 1 + groups - 1 + 5)

    for copy in x_first:
        copy.start()

    row, col = iota(0), iota(1)
    upto = jnp.where(row <= col, 1.0, 0.0).astype(BF16)
    rate = rate_ref[...]
    first, rest = split(rate)
    last = (rate - first.astype(F32) - rest.astype(F32)).astype(BF16)
    logs[...] = -(mm(first, upto) + (mm(rest, upto) + mm(last, upto)))
    for copy in loads[:3]:
        copy.wait()

    def map_copies(head, to):
        return [
            pltpu.make_async_remote_copy(
                src_ref=source.at[head],
                dst_ref=target.at[to],
                send_sem=send1.at[number, head],
                recv_sem=recv1.at[number, to],
                device_id=device(group, head),
                device_id_type=MESH,
            )
            for number, (source, target) in enumerate([(maps, maps_in), (adds, adds_in)])
        ]

    def map_keeps(head, to):
        return [
            pltpu.make_async_copy(maps.at[head], maps_in.at[to], recv1.at[0, to]),
            pltpu.make_async_copy(adds.at[head], adds_in.at[to], recv1.at[1, to]),
        ]

    def key_head(kh):
        columns = pl.ds(pl.multiple_of(kh * DK, DK), DK)
        k_raw, q_raw = k_ref[:, columns], q_ref[:, columns]
        k_wide, q_wide = k_raw.astype(F32), q_raw.astype(F32)
        k_inv = lax.rsqrt(jnp.sum(k_wide * k_wide, axis=1, keepdims=True) + 1e-6)
        q_inv = lax.rsqrt(jnp.sum(q_wide * q_wide, axis=1, keepdims=True) + 1e-6) * DK ** (-0.5)
        k_inv = jnp.broadcast_to(k_inv, (128, 128))
        k_inv_row = k_inv.T
        k_t = k_wide.T.astype(BF16)
        gram = mm_t(k_raw, k_raw) * k_inv * k_inv_row
        mixed = mm_t(q_raw, k_raw) * q_inv * k_inv_row
        for part in range(HV // HK):
            h = kh * (HV // HK) + part
            head_columns = pl.ds(pl.multiple_of(h * DV, DV), DV)
            log_row = rows_of(logs[pl.ds(h, 1), :])
            log_col = log_row.T
            beta_row = rows_of(beta_ref[pl.ds(h, 1), :])
            beta_col = beta_row.T
            ratio = jnp.where(row >= col, jnp.exp(jnp.where(row >= col, log_col - log_row, 0.0)), 0.0)
            inverse = unit_inverse(jnp.where(row > col, ratio * gram, 0.0) * beta_col)
            v_raw = v_ref[:, head_columns]
            weights = split(inverse * beta_row)
            newest = mm(weights[0], v_raw) + mm(weights[1], v_raw)
            weights = split(inverse * (beta_row * jnp.exp(log_row) * k_inv_row))
            key_matrix = mm(weights[0], k_raw) + mm(weights[1], k_raw)
            log_last = jnp.broadcast_to(logs[pl.ds(h, 1), 127:128], (128, 128))
            fade = k_inv * jnp.exp(log_last - log_col)
            side = split(key_matrix * fade)
            moved = mm(k_t, side[0]) + mm(k_t, side[1])
            maps[h] = jnp.where(row == col, jnp.exp(log_last), 0.0) - moved
            side = split(newest * fade)
            adds[h] = (mm(k_t, side[0]) + mm(k_t, side[1])).astype(BF16)
            mix = split(mixed * ratio)
            local_out[h] = mm3(mix, split(newest))
            effective = split(q_wide * q_inv * jnp.exp(log_col) - mm3(mix, split(key_matrix)))
            query_high[h] = effective[0]
            query_low[h] = effective[1]

    def key_heads(step, carry):
        for part in range(TOGETHER):
            key_head(step * TOGETHER + part)
        for part in range(TOGETHER * (HV // HK)):
            h = step * (TOGETHER * (HV // HK)) + part

            @pl.when(h != rank)
            def _():
                for copy in map_copies(h, rank):
                    copy.start()

            @pl.when(h == rank)
            def _():
                for copy in map_keeps(h, rank):
                    copy.start()

        @pl.when(step == 1)
        def _():
            for copy in x_landing[:2]:
                copy.wait()
            for copy in x_second + z_first[0] + z_first[1] + [across[0][0], across[1][0]]:
                copy.start()

        @pl.when(step == HK // TOGETHER - 2)
        def _():
            for copy in x_landing[2:]:
                copy.wait()
            for copy in z_first[2] + [across[2][0]]:
                copy.start()

        return carry

    lax.fori_loop(0, HK // TOGETHER, key_heads, 0)

    for number in range(3):
        for copy in z_landing[number][:2]:
            copy.wait()
        for copy in z_second[number] + [across[number][3], across[number][1]]:
            copy.start()

    for copy in map_keeps(0, 0):
        copy.wait()
    prefix[0] = maps_in[0]
    prefix_add[0] = adds_in[0].astype(F32)

    def chain(index, carry):
        for copy in map_keeps(index, index):
            copy.wait()
        step = split(maps_in[index])
        prefix[index] = mm3(step, split(prefix[index - 1]))
        prefix_add[index] = mm3(step, split(prefix_add[index - 1])) + adds_in[index].astype(F32)
        return carry

    lax.fori_loop(1, GROUP, chain, 0)
    last_add[...] = prefix_add[GROUP - 1].astype(BF16)

    def group_copies(to, source):
        return [
            pltpu.make_async_remote_copy(
                src_ref=kept,
                dst_ref=target.at[source],
                send_sem=send2.at[number, to],
                recv_sem=recv2.at[number, source],
                device_id=device(to, rank),
                device_id_type=MESH,
            )
            for number, (kept, target) in enumerate([(prefix.at[GROUP - 1], groups_in), (last_add, groups_add)])
        ]

    def send_group(to, carry):
        for copy in group_copies(to, group):
            copy.start()
        return carry

    lax.fori_loop(group + 1, groups, send_group, 0)

    for number in range(3):
        for copy in z_landing[number][2:]:
            copy.wait()
        across[number][2].start()

    def enter(source, state):
        for copy in group_copies(group, source):
            copy.wait_recv()
        return mm3(split(groups_in[source]), split(state)) + groups_add[source].astype(F32)

    entering = split(lax.fori_loop(0, group, enter, jnp.zeros((DK, DV), F32)))

    def state_copy(to, head):
        return pltpu.make_async_remote_copy(
            src_ref=states.at[to],
            dst_ref=states_in.at[head],
            send_sem=send3.at[to],
            recv_sem=recv3.at[head],
            device_id=device(group, to),
            device_id_type=MESH,
        )

    def state_keep(to, head):
        return pltpu.make_async_copy(states.at[to], states_in.at[head], recv3.at[head])

    def give(to):
        @pl.when(to != rank)
        def _():
            state_copy(to, rank).start()

        @pl.when(to == rank)
        def _():
            state_keep(to, rank).start()

    states[0] = entering[0]
    give(0)

    def spread(index, carry):
        moved = mm3(split(prefix[index - 1]), entering) + prefix_add[index - 1]
        states[index] = moved.astype(BF16)
        give(index)
        return carry

    lax.fori_loop(1, GROUP, spread, 0)

    gain = gain_ref[...]
    loads[3].wait()

    def finish(h, carry):
        columns = pl.ds(pl.multiple_of(h * DV, DV), DV)
        gate = gate_ref[:, columns].astype(F32)
        scale = gain * (gate / (1.0 + jnp.exp(-gate)))
        state_keep(h, h).wait()
        state = states_in[h]
        out = local_out[h] + (mm(query_high[h], state) + mm(query_low[h], state))
        inv_rms = lax.rsqrt(jnp.sum(out * out, axis=1, keepdims=True) * (1.0 / DV) + 1e-6)
        core_out[:, columns] = (out * inv_rms * scale).astype(BF16)
        return carry

    lax.fori_loop(0, HV, finish, 0)

    loads[4].wait()
    loads[5].wait()
    for number in range(3):
        for copy in across_landing[number]:
            copy.wait()
    width = proj_hbm.shape[1]

    def project(index, square):
        columns = pl.ds(pl.multiple_of(index * width, width), width)
        mixed = mm(core_out[...], proj[index])
        hidden = (residual_ref[:, columns].astype(F32) + mixed).astype(BF16)
        hidden_ref[:, columns] = hidden
        wide = hidden.astype(F32)
        return square + jnp.sum(wide * wide, axis=1, keepdims=True)

    square = lax.fori_loop(0, exp_size, project, jnp.zeros((128, 1), F32))
    inv_rms = lax.rsqrt(square * (1.0 / D) + 1e-6)
    normed_ref[...] = (hidden_ref[...].astype(F32) * inv_rms * post_gain_ref[...]).astype(BF16)

    def drain(index, carry):
        @pl.when(index != rank)
        def _():
            for copy in map_copies(index, rank):
                copy.wait_send()
            state_copy(index, rank).wait_send()

        return carry

    lax.fori_loop(0, GROUP, drain, 0)

    def drain_group(to, carry):
        for copy in group_copies(to, group):
            copy.wait_send()
        return carry

    lax.fori_loop(group + 1, groups, drain_group, 0)
    for copy in x_first + x_second:
        copy.wait_send()
    for number in range(3):
        for copy in z_first[number] + z_second[number] + across[number]:
            copy.wait_send()


def mixer(query, key, value, gate, residual, proj, strength, rate, head_gain, post_gain, stride):
    seq_size, exp_size = lax.axis_size("seq"), lax.axis_size("exp")
    groups = seq_size * exp_size // GROUP
    tokens = query.shape[0]
    vmem = pl.BlockSpec(memory_space=pltpu.VMEM)
    hbm = pl.BlockSpec(memory_space=pl.ANY)
    square = (128, 128)
    return pl.pallas_call(
        partial(mixer_kernel, seq_size, exp_size, stride),
        out_shape=[jax.ShapeDtypeStruct((tokens, D), BF16)] * 2,
        in_specs=[hbm] * 6 + [vmem] * 4,
        out_specs=[vmem, vmem],
        scratch_shapes=[
            pltpu.VMEM(query.shape, BF16),
            pltpu.VMEM(key.shape, BF16),
            pltpu.VMEM(value.shape, BF16),
            pltpu.VMEM(gate.shape, BF16),
            pltpu.VMEM(residual.shape, BF16),
            pltpu.VMEM((exp_size,) + proj.shape, BF16),
            pltpu.VMEM(value.shape, BF16),
            pltpu.VMEM((HV, tokens), F32),
            pltpu.VMEM((HV,) + square, F32),
            pltpu.VMEM((HV,) + square, BF16),
            pltpu.VMEM((HV,) + square, BF16),
            pltpu.VMEM((HV,) + square, F32),
            pltpu.VMEM((HV,) + square, BF16),
            pltpu.VMEM((GROUP,) + square, F32),
            pltpu.VMEM((GROUP,) + square, BF16),
            pltpu.VMEM((GROUP,) + square, F32),
            pltpu.VMEM((GROUP,) + square, F32),
            pltpu.VMEM(square, BF16),
            pltpu.VMEM((groups,) + square, F32),
            pltpu.VMEM((groups,) + square, BF16),
            pltpu.VMEM((GROUP,) + square, BF16),
            pltpu.VMEM((HV,) + square, BF16),
            pltpu.SemaphoreType.DMA((6,)),
            pltpu.SemaphoreType.DMA((2, HV)),
            pltpu.SemaphoreType.DMA((2, GROUP)),
            pltpu.SemaphoreType.DMA((2, groups)),
            pltpu.SemaphoreType.DMA((2, groups)),
            pltpu.SemaphoreType.DMA((GROUP,)),
            pltpu.SemaphoreType.DMA((HV,)),
            pltpu.SemaphoreType.DMA((28,)),
            pltpu.SemaphoreType.DMA((28,)),
        ],
        compiler_params=pltpu.CompilerParams(
            collective_id=0, has_side_effects=True, vmem_limit_bytes=56 * 1024 * 1024
        ),
        cost_estimate=pl.CostEstimate(flops=8_000_000_000, bytes_accessed=4_000_000, transcendentals=0),
    )(
        query,
        key,
        value,
        gate,
        residual,
        proj,
        rate.T,
        strength.T,
        head_gain.reshape(1, DV),
        post_gain.reshape(1, D),
    )


def slot_tables(expert_ids, gate_weights, experts, capacity):
    tokens = expert_ids.shape[0]
    named = expert_ids.T[:, None, :] == jnp.arange(experts, dtype=jnp.int32)[None, :, None]
    weight = jnp.sum(jnp.where(named, gate_weights.T[:, None, :], 0.0), axis=0)
    chosen = jnp.any(named, axis=0)
    earlier = jnp.arange(tokens)[:, None] < jnp.arange(tokens)[None, :]
    before = jnp.dot(chosen.astype(BF16), earlier.astype(BF16), preferred_element_type=F32).astype(jnp.int32)
    before = jnp.where(chosen, before, -1)
    here = before[:, None, :] == jnp.arange(capacity, dtype=jnp.int32)[None, :, None]
    pick = here.astype(BF16).reshape(experts * capacity, tokens)
    mix = jnp.where(here, weight[:, None, :], 0.0).reshape(experts * capacity, tokens)
    return pick, mix


def shards(
    residual_in,
    query_input,
    key_input,
    value_input,
    out_gate,
    write_strength,
    decay_rate,
    head_gain,
    out_proj,
    post_gain,
    expert_ids,
    gate_weights,
    expert_gate,
    expert_up,
    expert_down,
):
    tokens = residual_in.shape[0]
    devices = lax.axis_size(("seq", "exp"))
    local_experts = expert_gate.shape[0]
    experts = local_experts * devices
    capacity = max(2, tokens * TOP * 8 // (5 * experts))
    pick, mix = slot_tables(expert_ids, gate_weights, experts, capacity)
    both_axes = ("seq", "exp")
    stride = lax.axis_size("seq") // 4
    hidden_state, normed = mixer(
        query_input,
        key_input,
        value_input,
        out_gate,
        residual_in,
        out_proj,
        write_strength,
        decay_rate,
        head_gain,
        post_gain,
        stride,
    )
    pick = pick.reshape(devices, local_experts, capacity, tokens)
    returned = []
    arrived = []
    for e in range(local_experts):
        send = jnp.dot(pick[:, e].reshape(devices * capacity, tokens), normed, preferred_element_type=F32).astype(BF16)
        send = send.reshape(devices, capacity, D)
        arrived.append(lax.all_to_all(send, both_axes, split_axis=0, concat_axis=0, tiled=True))
    for e in range(local_experts):
        block = arrived[e].reshape(devices * capacity, D)
        gate_part = jnp.dot(block, expert_gate[e], preferred_element_type=F32)
        up_part = jnp.dot(block, expert_up[e], preferred_element_type=F32)
        inner = (gate_part / (1.0 + jnp.exp(-gate_part)) * up_part).astype(BF16)
        result = jnp.dot(inner, expert_down[e], preferred_element_type=F32).astype(BF16)
        result = result.reshape(devices, capacity, D)
        returned.append(lax.all_to_all(result, both_axes, split_axis=0, concat_axis=0, tiled=True))
    mix_high = mix.astype(BF16)
    mix_low = (mix - mix_high.astype(F32)).astype(BF16)
    mix = jnp.concatenate([mix_high, mix_low], axis=1).reshape(devices, local_experts, capacity, 2 * tokens)
    routed = 0.0
    for e in range(local_experts):
        both = lax.dot_general(
            mix[:, e].reshape(devices * capacity, 2 * tokens),
            returned[e].reshape(devices * capacity, D),
            (((0,), (0,)), ((), ())),
            preferred_element_type=F32,
        )
        routed = routed + (both[:tokens] + both[tokens:])
    return (hidden_state.astype(F32) + routed).astype(BF16)


def solution(mesh):
    both = ("seq", "exp")
    placed = (
        P(both, None),
        P(both, None),
        P(both, None),
        P(both, None),
        P(both, None),
        P(both, None),
        P(both, None),
        P(),
        P(None, "exp"),
        P(),
        P(both, None),
        P(both, None),
        P(both, None, None),
        P(both, None, None),
        P(both, None, None),
    )
    return jax.shard_map(shards, mesh=mesh, in_specs=placed, out_specs=P(both, None), check_vma=False)
```

```python
from functools import partial

import jax
import jax.numpy as jnp
from jax import lax
from jax.experimental import pallas as pl
from jax.experimental.pallas import tpu as pltpu
from jax.sharding import PartitionSpec as P

D = 2048
HK = 8
HV = 16
DK = 128
DV = 128
TOP = 10
TOGETHER = 1
GROUP = 16

F32 = jnp.float32
BF16 = jnp.bfloat16
MESH = pl.DeviceIdType.MESH


def mm(a, b):
    return jnp.dot(a, b, preferred_element_type=F32)


def mm_t(a, b):
    return lax.dot_general(a, b, (((1,), (1,)), ((), ())), preferred_element_type=F32)


def split(x):
    high = x.astype(BF16)
    return high, (x - high.astype(F32)).astype(BF16)


def mm3(a, b):
    return mm(a[0], b[1]) + mm(jnp.concatenate([a[0], a[1]], axis=1), jnp.concatenate([b[0], b[0]], axis=0))


def mm2(a, b):
    return mm(a[0], b) + mm(a[1], b)


def iota(axis):
    return lax.broadcasted_iota(jnp.int32, (128, 128), axis)


def rows_of(row):
    return jnp.broadcast_to(row, (128, 128))


def unit_inverse(lower):
    row, col = iota(0), iota(1)
    eye = jnp.where(row == col, 1.0, 0.0)
    inverse = eye - jnp.where((row >> 1) == (col >> 1), lower, 0.0)
    for level in range(1, 7):
        mask = ((row >> (level + 1)) == (col >> (level + 1))) & ((row >> level) != (col >> level))
        part = split(jnp.where(mask, lower, 0.0))
        blocks = split(inverse)
        inverse = inverse - mm3(blocks, split(mm3(part, blocks)))
    return inverse


def mixer_kernel(
    seq_size,
    exp_size,
    stride,
    q_hbm,
    k_hbm,
    v_hbm,
    gate_hbm,
    residual_hbm,
    proj_hbm,
    rate_ref,
    beta_ref,
    gain_ref,
    post_gain_ref,
    hidden_ref,
    normed_ref,
    q_ref,
    k_ref,
    v_ref,
    gate_ref,
    residual_ref,
    proj,
    core_out,
    logs,
    local_out,
    query_high,
    query_low,
    maps,
    adds,
    maps_in,
    adds_in,
    prefix,
    prefix_add,
    last_map,
    last_add,
    groups_in,
    groups_add,
    states,
    states_in,
    load,
    send1,
    recv1,
    send2,
    recv2,
    send3,
    recv3,
    proj_send,
    proj_recv,
):
    lines = GROUP // exp_size
    groups = seq_size // lines
    seq, exp = lax.axis_index("seq"), lax.axis_index("exp")
    group = seq // lines
    rank = (seq % lines) * exp_size + exp

    loads = [
        pltpu.make_async_copy(source, target, load.at[number])
        for number, (source, target) in enumerate(
            [
                (k_hbm, k_ref),
                (q_hbm, q_ref),
                (v_hbm, v_ref),
                (gate_hbm, gate_ref),
                (residual_hbm, residual_ref),
                (proj_hbm, proj.at[exp]),
            ]
        )
    ]
    for copy in loads:
        copy.start()

    def device(of_group, of_rank):
        return (of_group * lines + of_rank // exp_size, of_rank % exp_size)

    core = seq % 2
    spot = (seq // stride) % 4

    def ring_seq(shift):
        return seq + ((spot + shift) % 4 - spot) * stride

    def ring_exp(shift):
        return lax.rem(exp + shift, 4)

    partner = (seq + 1 - 2 * core, exp)
    rows = proj_hbm.shape[0] // 8
    half = rows // 2

    def piece(x_shift, spot_shift, begin, size):
        row = pl.multiple_of(core * (4 * rows) + (spot + spot_shift) % 4 * rows + begin, half)
        return proj.at[ring_exp(x_shift), pl.ds(row, size)]

    counter = [0]

    def proj_copy(ref, recv_index, to, source=None):
        number = counter[0]
        counter[0] += 1
        return pltpu.make_async_remote_copy(
            src_ref=ref if source is None else source,
            dst_ref=ref,
            send_sem=proj_send.at[number],
            recv_sem=proj_recv.at[recv_index],
            device_id=to,
            device_id_type=MESH,
        )

    def landing(ref, recv_index):
        return pltpu.make_async_copy(ref, ref, proj_recv.at[recv_index])

    own = proj_hbm.at[pl.ds(pl.multiple_of(core * (4 * rows) + spot * rows, half), rows)]
    mine = piece(0, 0, 0, rows)
    right, left = (seq, ring_exp(1)), (seq, ring_exp(3))
    above, below = (ring_seq(1), exp), (ring_seq(3), exp)
    x_first = [proj_copy(mine, 0, right, own), proj_copy(mine, 1, left, own)]
    x_second = [proj_copy(piece(3, 0, 0, half), 2, right), proj_copy(piece(1, 0, half, half), 3, left)]
    x_landing = [
        landing(piece(3, 0, 0, rows), 0),
        landing(piece(1, 0, 0, rows), 1),
        landing(piece(2, 0, 0, half), 2),
        landing(piece(2, 0, half, half), 3),
    ]
    shifts = (3, 1, 2)
    z_first, z_second, z_landing, across, across_landing = [], [], [], [], []
    for number, shift in enumerate(shifts):
        at = 4 + 4 * number
        z_first.append(
            [proj_copy(piece(shift, 0, 0, rows), at, above), proj_copy(piece(shift, 0, 0, rows), at + 1, below)]
        )
        z_second.append(
            [proj_copy(piece(shift, 3, 0, half), at + 2, above), proj_copy(piece(shift, 1, half, half), at + 3, below)]
        )
        z_landing.append(
            [
                landing(piece(shift, 3, 0, rows), at),
                landing(piece(shift, 1, 0, rows), at + 1),
                landing(piece(shift, 2, 0, half), at + 2),
                landing(piece(shift, 2, half, half), at + 3),
            ]
        )
        across.append([proj_copy(piece(shift, n, 0, rows), 16 + 4 * number + n, partner) for n in range(4)])
        other = (1 - core) * (4 * rows)
        across_landing.append(
            [
                landing(
                    proj.at[
                        ring_exp(shift), pl.ds(pl.multiple_of(other + (spot + n) % 4 * rows, half), rows)
                    ],
                    16 + 4 * number + n,
                )
                for n in range(4)
            ]
        )

    barrier = pltpu.get_barrier_semaphore()

    def greet(to):
        pl.semaphore_signal(barrier, inc=1, device_id=to, device_id_type=MESH)

    def greet_rank(step, carry):
        greet(device(group, lax.rem(rank + step, GROUP)))
        return carry

    def greet_group(step, carry):
        greet(device(lax.rem(group + step, groups), rank))
        return carry

    lax.fori_loop(1, GROUP, greet_rank, 0)
    lax.fori_loop(1, groups, greet_group, 0)
    for to in (right, left, above, below, partner):
        greet(to)
    pl.semaphore_wait(barrier, GROUP - 1 + groups - 1 + 5)

    for copy in x_first:
        copy.start()

    row, col = iota(0), iota(1)
    upto = jnp.where(row <= col, 1.0, 0.0).astype(BF16)
    rate = rate_ref[...]
    first, rest = split(rate)
    last = (rate - first.astype(F32) - rest.astype(F32)).astype(BF16)
    logs[...] = -(mm(first, upto) + (mm(rest, upto) + mm(last, upto)))
    for copy in loads[:3]:
        copy.wait()

    def map_copies(head, to):
        return [
            pltpu.make_async_remote_copy(
                src_ref=source.at[head],
                dst_ref=target.at[to],
                send_sem=send1.at[number, head],
                recv_sem=recv1.at[number, to],
                device_id=device(group, head),
                device_id_type=MESH,
            )
            for number, (source, target) in enumerate([(maps, maps_in), (adds, adds_in)])
        ]

    def map_keeps(head, to):
        return [
            pltpu.make_async_copy(maps.at[head], maps_in.at[to], recv1.at[0, to]),
            pltpu.make_async_copy(adds.at[head], adds_in.at[to], recv1.at[1, to]),
        ]

    def key_head(kh):
        columns = pl.ds(pl.multiple_of(kh * DK, DK), DK)
        k_raw, q_raw = k_ref[:, columns], q_ref[:, columns]
        k_wide, q_wide = k_raw.astype(F32), q_raw.astype(F32)
        k_inv = lax.rsqrt(jnp.sum(k_wide * k_wide, axis=1, keepdims=True) + 1e-6)
        q_inv = lax.rsqrt(jnp.sum(q_wide * q_wide, axis=1, keepdims=True) + 1e-6) * DK ** (-0.5)
        k_inv = jnp.broadcast_to(k_inv, (128, 128))
        k_inv_row = k_inv.T
        k_t = k_wide.T.astype(BF16)
        gram = mm_t(k_raw, k_raw) * k_inv * k_inv_row
        mixed = mm_t(q_raw, k_raw) * q_inv * k_inv_row
        for part in range(HV // HK):
            h = kh * (HV // HK) + part
            head_columns = pl.ds(pl.multiple_of(h * DV, DV), DV)
            log_row = rows_of(logs[pl.ds(h, 1), :])
            log_col = log_row.T
            beta_row = rows_of(beta_ref[pl.ds(h, 1), :])
            beta_col = beta_row.T
            ratio = jnp.where(row >= col, jnp.exp(jnp.where(row >= col, log_col - log_row, 0.0)), 0.0)
            inverse = unit_inverse(jnp.where(row > col, ratio * gram, 0.0) * beta_col)
            v_raw = v_ref[:, head_columns]
            weights = split(inverse * beta_row)
            newest = mm2(weights, v_raw)
            weights = split(inverse * (beta_row * jnp.exp(log_row) * k_inv_row))
            key_matrix = mm2(weights, k_raw)
            log_last = jnp.broadcast_to(logs[pl.ds(h, 1), 127:128], (128, 128))
            fade = k_inv * jnp.exp(log_last - log_col)
            side = split(key_matrix * fade)
            moved = mm(k_t, side[0]) + mm(k_t, side[1])
            maps[h] = jnp.where(row == col, jnp.exp(log_last), 0.0) - moved
            side = split(newest * fade)
            adds[h] = (mm(k_t, side[0]) + mm(k_t, side[1])).astype(BF16)
            mix = split(mixed * ratio)
            local_out[h] = mm3(mix, split(newest))
            effective = split(q_wide * q_inv * jnp.exp(log_col) - mm3(mix, split(key_matrix)))
            query_high[h] = effective[0]
            query_low[h] = effective[1]

    def key_heads(step, carry):
        for part in range(TOGETHER):
            key_head(step * TOGETHER + part)
        for part in range(TOGETHER * (HV // HK)):
            h = step * (TOGETHER * (HV // HK)) + part

            @pl.when(h != rank)
            def _():
                for copy in map_copies(h, rank):
                    copy.start()

            @pl.when(h == rank)
            def _():
                for copy in map_keeps(h, rank):
                    copy.start()

        @pl.when(step == 1)
        def _():
            for copy in x_landing[:2]:
                copy.wait()
            for copy in x_second + z_first[0] + z_first[1] + [across[0][0], across[1][0]]:
                copy.start()

        @pl.when(step == HK // TOGETHER - 2)
        def _():
            for copy in x_landing[2:]:
                copy.wait()
            for copy in z_first[2] + [across[2][0]]:
                copy.start()

        return carry

    lax.fori_loop(0, HK // TOGETHER, key_heads, 0)

    for number in range(3):
        for copy in z_landing[number][:2]:
            copy.wait()
        for copy in z_second[number] + [across[number][3], across[number][1]]:
            copy.start()

    middle = GROUP // 2
    for start in (0, middle):
        for copy in map_keeps(start, start):
            copy.wait()
        prefix[start] = maps_in[start]
        prefix_add[start] = adds_in[start].astype(F32)

    def chain(step, carry):
        for start in (0, middle):
            index = start + step
            for copy in map_keeps(index, index):
                copy.wait()
        for start in (0, middle):
            index = start + step
            moved = split(maps_in[index])
            prefix[index] = mm3(moved, split(prefix[index - 1]))
            prefix_add[index] = mm3(moved, split(prefix_add[index - 1])) + adds_in[index].astype(F32)
        return carry

    lax.fori_loop(1, middle, chain, 0)
    moved = split(prefix[GROUP - 1])
    last_map[...] = mm3(moved, split(prefix[middle - 1]))
    last_add[...] = (mm3(moved, split(prefix_add[middle - 1])) + prefix_add[GROUP - 1]).astype(BF16)

    def group_copies(to, source):
        return [
            pltpu.make_async_remote_copy(
                src_ref=kept,
                dst_ref=target.at[source],
                send_sem=send2.at[number, to],
                recv_sem=recv2.at[number, source],
                device_id=device(to, rank),
                device_id_type=MESH,
            )
            for number, (kept, target) in enumerate([(last_map, groups_in), (last_add, groups_add)])
        ]

    def send_group(to, carry):
        for copy in group_copies(to, group):
            copy.start()
        return carry

    lax.fori_loop(group + 1, groups, send_group, 0)

    for number in range(3):
        for copy in z_landing[number][2:]:
            copy.wait()
        across[number][2].start()

    def enter(source, state):
        for copy in group_copies(group, source):
            copy.wait_recv()
        return mm3(split(groups_in[source]), split(state)) + groups_add[source].astype(F32)

    entering = split(lax.fori_loop(0, group, enter, jnp.zeros((DK, DV), F32)))
    halfway = split(mm3(split(prefix[middle - 1]), entering) + prefix_add[middle - 1])

    def state_copy(to, head):
        return pltpu.make_async_remote_copy(
            src_ref=states.at[to],
            dst_ref=states_in.at[head],
            send_sem=send3.at[to],
            recv_sem=recv3.at[head],
            device_id=device(group, to),
            device_id_type=MESH,
        )

    def state_keep(to, head):
        return pltpu.make_async_copy(states.at[to], states_in.at[head], recv3.at[head])

    def give(to):
        @pl.when(to != rank)
        def _():
            state_copy(to, rank).start()

        @pl.when(to == rank)
        def _():
            state_keep(to, rank).start()

    states[0] = entering[0]
    states[middle] = halfway[0]
    give(0)
    give(middle)

    def spread(step, carry):
        for start, state in ((0, entering), (middle, halfway)):
            index = start + step
            moved = mm3(split(prefix[index - 1]), state) + prefix_add[index - 1]
            states[index] = moved.astype(BF16)
        for start in (0, middle):
            give(start + step)
        return carry

    lax.fori_loop(1, middle, spread, 0)

    gain = gain_ref[...]
    loads[3].wait()

    def finish(h, carry):
        columns = pl.ds(pl.multiple_of(h * DV, DV), DV)
        gate = gate_ref[:, columns].astype(F32)
        scale = gain * (gate / (1.0 + jnp.exp(-gate)))
        state_keep(h, h).wait()
        state = states_in[h]
        out = local_out[h] + (mm(query_high[h], state) + mm(query_low[h], state))
        inv_rms = lax.rsqrt(jnp.sum(out * out, axis=1, keepdims=True) * (1.0 / DV) + 1e-6)
        core_out[:, columns] = (out * inv_rms * scale).astype(BF16)
        return carry

    lax.fori_loop(0, HV, finish, 0, unroll=4)

    loads[4].wait()
    loads[5].wait()
    for number in range(3):
        for copy in across_landing[number]:
            copy.wait()
    width = proj_hbm.shape[1]

    def project(index, square):
        columns = pl.ds(pl.multiple_of(index * width, width), width)
        mixed = mm(core_out[...], proj[index])
        hidden = (residual_ref[:, columns].astype(F32) + mixed).astype(BF16)
        hidden_ref[:, columns] = hidden
        wide = hidden.astype(F32)
        return square + jnp.sum(wide * wide, axis=1, keepdims=True)

    square = lax.fori_loop(0, exp_size, project, jnp.zeros((128, 1), F32))
    inv_rms = lax.rsqrt(square * (1.0 / D) + 1e-6)
    normed_ref[...] = (hidden_ref[...].astype(F32) * inv_rms * post_gain_ref[...]).astype(BF16)

    def drain(index, carry):
        @pl.when(index != rank)
        def _():
            for copy in map_copies(index, rank):
                copy.wait_send()
            state_copy(index, rank).wait_send()

        return carry

    lax.fori_loop(0, GROUP, drain, 0)

    def drain_group(to, carry):
        for copy in group_copies(to, group):
            copy.wait_send()
        return carry

    lax.fori_loop(group + 1, groups, drain_group, 0)
    for copy in x_first + x_second:
        copy.wait_send()
    for number in range(3):
        for copy in z_first[number] + z_second[number] + across[number]:
            copy.wait_send()


def mixer(query, key, value, gate, residual, proj, strength, rate, head_gain, post_gain, stride):
    seq_size, exp_size = lax.axis_size("seq"), lax.axis_size("exp")
    groups = seq_size * exp_size // GROUP
    tokens = query.shape[0]
    vmem = pl.BlockSpec(memory_space=pltpu.VMEM)
    hbm = pl.BlockSpec(memory_space=pl.ANY)
    square = (128, 128)
    return pl.pallas_call(
        partial(mixer_kernel, seq_size, exp_size, stride),
        out_shape=[jax.ShapeDtypeStruct((tokens, D), BF16)] * 2,
        in_specs=[hbm] * 6 + [vmem] * 4,
        out_specs=[vmem, vmem],
        scratch_shapes=[
            pltpu.VMEM(query.shape, BF16),
            pltpu.VMEM(key.shape, BF16),
            pltpu.VMEM(value.shape, BF16),
            pltpu.VMEM(gate.shape, BF16),
            pltpu.VMEM(residual.shape, BF16),
            pltpu.VMEM((exp_size,) + proj.shape, BF16),
            pltpu.VMEM(value.shape, BF16),
            pltpu.VMEM((HV, tokens), F32),
            pltpu.VMEM((HV,) + square, F32),
            pltpu.VMEM((HV,) + square, BF16),
            pltpu.VMEM((HV,) + square, BF16),
            pltpu.VMEM((HV,) + square, F32),
            pltpu.VMEM((HV,) + square, BF16),
            pltpu.VMEM((GROUP,) + square, F32),
            pltpu.VMEM((GROUP,) + square, BF16),
            pltpu.VMEM((GROUP,) + square, F32),
            pltpu.VMEM((GROUP,) + square, F32),
            pltpu.VMEM(square, F32),
            pltpu.VMEM(square, BF16),
            pltpu.VMEM((groups,) + square, F32),
            pltpu.VMEM((groups,) + square, BF16),
            pltpu.VMEM((GROUP,) + square, BF16),
            pltpu.VMEM((HV,) + square, BF16),
            pltpu.SemaphoreType.DMA((6,)),
            pltpu.SemaphoreType.DMA((2, HV)),
            pltpu.SemaphoreType.DMA((2, GROUP)),
            pltpu.SemaphoreType.DMA((2, groups)),
            pltpu.SemaphoreType.DMA((2, groups)),
            pltpu.SemaphoreType.DMA((GROUP,)),
            pltpu.SemaphoreType.DMA((HV,)),
            pltpu.SemaphoreType.DMA((28,)),
            pltpu.SemaphoreType.DMA((28,)),
        ],
        compiler_params=pltpu.CompilerParams(
            collective_id=0, has_side_effects=True, vmem_limit_bytes=56 * 1024 * 1024
        ),
        cost_estimate=pl.CostEstimate(flops=8_000_000_000, bytes_accessed=4_000_000, transcendentals=0),
    )(
        query,
        key,
        value,
        gate,
        residual,
        proj,
        rate.T,
        strength.T,
        head_gain.reshape(1, DV),
        post_gain.reshape(1, D),
    )


PARTS = ((0, 1, 2), (1, 2, 0), (2, 0, 1))
BEGIN = (0, 640, 1280)
WIDTH = (640, 640, 768)
EXTRA = 8
BLOCK = 128 + EXTRA


class Torus:
    def __init__(self):
        seq, self.exp = lax.axis_index("seq"), lax.axis_index("exp")
        self.core = seq % 2
        self.at = (self.exp, (seq // 2) % 4, seq // 8)

    def place(self, axis, shift, core=None):
        x, y, z = [(c + shift) % 4 if n == axis else c for n, c in enumerate(self.at)]
        return ((z * 4 + y) * 2 + (self.core if core is None else core), x)

    def partner(self):
        return self.place(0, 0, 1 - self.core)

    def greet(self):
        barrier = pltpu.get_barrier_semaphore()
        others = [self.partner()]
        for axis in range(3):
            for shift in (1, 3):
                others += [self.place(axis, shift), self.place(axis, shift, 1 - self.core)]
        for to in others:
            pl.semaphore_signal(barrier, inc=1, device_id=to, device_id_type=MESH)
        pl.semaphore_wait(barrier, len(others))


class Sends:
    def __init__(self, send, recv):
        self.send, self.recv, self.count, self.open = send, recv, 0, []

    def go(self, source, target, index, to):
        copy = pltpu.make_async_remote_copy(
            src_ref=source,
            dst_ref=target,
            send_sem=self.send.at[self.count],
            recv_sem=self.recv.at[index],
            device_id=to,
            device_id_type=MESH,
        )
        self.count += 1
        copy.start()
        self.open.append(copy)

    def keep(self, source, target, index):
        pltpu.make_async_copy(source, target, self.recv.at[index]).start()

    def landed(self, target, index):
        pltpu.make_async_copy(target, target, self.recv.at[index]).wait()

    def finish(self):
        for copy in self.open:
            copy.wait_send()


def view(ref, expert, core, columns, chosen):
    x, y, z = [chosen.get(axis, slice(None)) for axis in range(3)]
    return ref.at[z, expert, x, y, core, slice(None), columns]


def ordered(part, second, first):
    return (second, first) if part == 0 else (first, second)


def slots(expert):
    return pl.ds(8 * expert, 8)


def dispatch_kernel(normed_ref, ids_ref, weight_ref, out_ref, mix_ref, extra, *scratch):
    blocks, rows_out = scratch[0:3], scratch[3:6]
    from_left, from_right = scratch[6:9], scratch[9:12]
    sends = Sends(scratch[12], scratch[13])
    torus = Torus()
    extra[...] = jnp.full(extra.shape, -1.0, F32)
    extra[0, :TOP] = ids_ref[...].astype(F32)
    extra[1, :TOP] = weight_ref[...]
    for p in range(3):
        columns = pl.ds(BEGIN[p], WIDTH[p])
        blocks[p][0, 0, :128, :] = normed_ref[:, columns]
        for number in range(4):
            lanes = slice(128 * number, 128 * (number + 1))
            rows = slice(8 * (number % 2), 8 * (number % 2) + 8)
            blocks[p][0, 0, 128:, lanes] = extra[number // 2, rows].astype(BF16)
        blocks[p][0, 0, 128:, 512:] = jnp.zeros((EXTRA, WIDTH[p] - 512), BF16)
    torus.greet()
    low, high = pl.ds(0, 72), pl.ds(72, BLOCK - 72)

    def hand_on(p, first):
        b = PARTS[p][2]
        block = blocks[p].at[0, first]
        sends.go(block, blocks[p].at[3, first], 64 * p + 4 + first, torus.place(b, 1))
        sends.go(block, blocks[p].at[1, first], 64 * p + 8 + first, torus.place(b, 3))

    def gathered(p, second, first):
        sends.landed(blocks[p].at[second, first], 64 * p + (4 if second == 3 else 8) + first)

    for p, (_, a, b) in enumerate(PARTS):
        own = blocks[p].at[0, 0]
        sends.go(own, blocks[p].at[0, 3], 64 * p + 0, torus.place(a, 1))
        sends.go(own, blocks[p].at[0, 1], 64 * p + 1, torus.place(a, 3))
    for p in range(3):
        hand_on(p, 0)
    for p, (_, a, b) in enumerate(PARTS):
        sends.landed(blocks[p].at[0, 3], 64 * p + 0)
        sends.go(blocks[p].at[0, 3, low], blocks[p].at[0, 2, low], 64 * p + 2, torus.place(a, 1))
        sends.landed(blocks[p].at[0, 1], 64 * p + 1)
        sends.go(blocks[p].at[0, 1, high], blocks[p].at[0, 2, high], 64 * p + 3, torus.place(a, 3))
        hand_on(p, 1)
        hand_on(p, 3)
    for p in range(3):
        sends.landed(blocks[p].at[0, 2, low], 64 * p + 2)
        sends.landed(blocks[p].at[0, 2, high], 64 * p + 3)
        hand_on(p, 2)

    row, col = iota(0), iota(1)
    earlier = jnp.where(row < col, 1.0, 0.0).astype(BF16)
    spread_row = lax.broadcasted_iota(jnp.int32, (128, 16), 0)
    spread_col = lax.broadcasted_iota(jnp.int32, (128, 16), 1)
    spread = jnp.where((spread_row >> 3) == spread_col, 1.0, 0.0).astype(BF16)
    slot = (row & 7).astype(F32)
    line = lax.broadcasted_iota(jnp.int32, (16, 128), 0)

    def extract(p, second):
        place = [(c + (line >> 2)) & 3 if n == PARTS[p][0] else c for n, c in enumerate(torus.at)]
        device = ((place[2] * 4 + place[1]) * 2 + ((line >> 1) & 1)) * 4 + place[0]
        expert = (device * 2 + (line & 1)).astype(F32)

        def one(first, carry):
            block = blocks[p].at[second, first]
            extras = [block[128:, 128 * n : 128 * (n + 1)].astype(F32) for n in range(4)]
            named = jnp.zeros((16, 128), F32)
            weight = jnp.zeros((16, 128), F32)
            for choice in range(TOP):
                number, at = choice // 8, slice(choice % 8, choice % 8 + 1)
                hit = expert == jnp.broadcast_to(extras[number][at, :], (16, 128))
                named = jnp.where(hit, 1.0, named)
                weight = jnp.where(hit, jnp.broadcast_to(extras[2 + number][at, :], (16, 128)), weight)
            before = mm(named.astype(BF16), earlier)
            code = jnp.where(named > 0.5, before, -1.0).astype(BF16)
            here = mm(spread, code) == slot
            pick = jnp.where(here, 1.0, 0.0).astype(BF16)
            mix = jnp.where(here, mm(spread, weight.astype(BF16)), 0.0)
            mix_ref[p, second * 4 + first] = mix.T.astype(BF16)
            taken = mm(pick, block[:128, :]).astype(BF16).reshape(8, 16, WIDTH[p])
            i, k = ordered(p, second, first)
            rows_out[p][:, i, k] = taken
            return carry

        lax.fori_loop(0, 4, one, 0, unroll=True)

    core = torus.core

    def chunk(p, second):
        return (second,) if p == 0 else (slice(None), second)

    def slot_of(p, place, of_core, second):
        return 64 * p + 24 + place * 8 + of_core * 4 + second

    def columns_of(p):
        return pl.ds(BEGIN[p], WIDTH[p])

    def every(p):
        return (slice(None),) if p == 0 else ()

    def send_chunk(p, second):
        axis, _, b = PARTS[p]
        rows = rows_out[p]
        for number, (relay, shift) in enumerate(((from_left[p], 1), (from_right[p], 3))):
            sends.go(
                rows.at[(4 + number,) + chunk(p, second)],
                relay.at[chunk(p, second)],
                64 * p + 14 + number * 4 + second,
                torus.place(axis, shift),
            )
        for e in range(2):

            def source(line):
                return rows.at[(line,) + chunk(p, second) + every(p) + (slots(e),)]

            for shift in (1, 3):
                for to_core in range(2):
                    sends.go(
                        source(2 * shift + to_core),
                        view(out_ref, e, core, columns_of(p), {axis: 4 - shift, b: second}),
                        slot_of(p, 4 - shift, core, second),
                        torus.place(axis, shift, to_core),
                    )
            here = view(out_ref, e, core, columns_of(p), {axis: 0, b: second})
            sends.go(source(1 - core), here, slot_of(p, 0, core, second), torus.partner())
            sends.keep(source(core), here, slot_of(p, 0, core, second))

    def pass_on(p, second):
        axis, _, b = PARTS[p]
        for number, (relay, shift) in enumerate(((from_left[p], 1), (from_right[p], 3))):
            sends.landed(relay.at[chunk(p, second)], 64 * p + 14 + number * 4 + second)
            for e in range(2):
                sends.go(
                    relay.at[chunk(p, second) + every(p) + (slots(e),)],
                    view(out_ref, e, core, columns_of(p), {axis: 2, b: second}),
                    slot_of(p, 2, core, second),
                    torus.place(axis, shift, number),
                )

    for p in range(3):
        extract(p, 0)
        send_chunk(p, 0)
    for p, (_, a, b) in enumerate(PARTS):
        gathered(p, 3, 0)
        gathered(p, 3, 1)
        sends.go(blocks[p].at[3, 0:2], blocks[p].at[2, 0:2], 64 * p + 12, torus.place(b, 1))
        gathered(p, 1, 3)
        gathered(p, 1, 2)
        sends.go(blocks[p].at[1, 2:4], blocks[p].at[2, 2:4], 64 * p + 13, torus.place(b, 3))
    for p in range(3):
        gathered(p, 3, 3)
        gathered(p, 3, 2)
        extract(p, 3)
        send_chunk(p, 3)
    for p in range(3):
        gathered(p, 1, 0)
        gathered(p, 1, 1)
        extract(p, 1)
        send_chunk(p, 1)
        pass_on(p, 0)
    for p in range(3):
        sends.landed(blocks[p].at[2, 0:2], 64 * p + 12)
        sends.landed(blocks[p].at[2, 2:4], 64 * p + 13)
        extract(p, 2)
        send_chunk(p, 2)
        pass_on(p, 3)
    for second in (1, 2):
        for p in range(3):
            pass_on(p, second)
    both = slice(None)
    for p, (axis, a, b) in enumerate(PARTS):
        for place in range(4):
            for of_core in range(2):
                for second in range(4):
                    sends.landed(
                        view(out_ref, both, of_core, columns_of(p), {axis: place, b: second}),
                        slot_of(p, place, of_core, second),
                    )
    sends.finish()


def dispatch(normed, ids, weights):
    vmem = pl.BlockSpec(memory_space=pltpu.VMEM)
    hbm = pl.BlockSpec(memory_space=pl.ANY)
    return pl.pallas_call(
        dispatch_kernel,
        out_shape=[
            jax.ShapeDtypeStruct((4, 2, 4, 4, 2, 8, D), BF16),
            jax.ShapeDtypeStruct((3, 16, 128, 128), BF16),
        ],
        in_specs=[vmem] * 3,
        out_specs=[hbm, vmem],
        scratch_shapes=[pltpu.VMEM((2, 16, 128), F32)]
        + [pltpu.VMEM((4, 4, BLOCK, w), BF16) for w in WIDTH]
        + [pltpu.VMEM((8, 4, 4, 16, w), BF16) for w in WIDTH]
        + [pltpu.VMEM((4, 4, 16, w), BF16) for w in WIDTH] * 2
        + [pltpu.SemaphoreType.DMA((240,)), pltpu.SemaphoreType.DMA((192,))],
        compiler_params=pltpu.CompilerParams(
            collective_id=1, has_side_effects=True, vmem_limit_bytes=58 * 1024 * 1024
        ),
        cost_estimate=pl.CostEstimate(flops=2_000_000_000, bytes_accessed=10_000_000, transcendentals=0),
    )(normed, ids, weights)


CHUNKS = (2, 1, 3, 0)


def combine_kernel(
    rows_hbm,
    gate_hbm,
    up_hbm,
    down_hbm,
    mix_ref,
    hidden_ref,
    out_ref,
    rows_ref,
    inner_ref,
    gate_ref,
    up_ref,
    down_ref,
    load,
    fetch,
    *scratch,
):
    rows_in, from_left, from_right = scratch[0:3], scratch[3:6], scratch[6:9]
    sums, over, under, add_over, add_under = (
        scratch[9:12],
        scratch[12:15],
        scratch[15:18],
        scratch[18:21],
        scratch[21:24],
    )
    sends = Sends(scratch[24], scratch[25])
    torus = Torus()
    core = torus.core
    loads = [pltpu.make_async_copy(rows_hbm.at[k], rows_ref.at[k], load.at[k]) for k in range(4)]
    weights = [
        [
            pltpu.make_async_copy(source.at[e], target.at[e], fetch.at[number, e])
            for number, (source, target) in enumerate(((gate_hbm, gate_ref), (up_hbm, up_ref), (down_hbm, down_ref)))
        ]
        for e in range(2)
    ]
    loads[CHUNKS[0]].start()
    for copy in weights[0] + weights[1]:
        copy.start()
    for k in CHUNKS[1:]:
        loads[k].start()
    torus.greet()

    def expert(k, e):
        if k == CHUNKS[0]:
            for copy in weights[e]:
                copy.wait()
        block = rows_ref.at[k, e].reshape(256, D)

        def widen(step, carry):
            columns = pl.ds(pl.multiple_of(step * 256, 256), 256)
            gate_part = mm(block[...], gate_ref[e, :, columns])
            up_part = mm(block[...], up_ref[e, :, columns])
            inner_ref[:, columns] = (gate_part / (1.0 + jnp.exp(-gate_part)) * up_part).astype(BF16)
            return carry

        lax.fori_loop(0, 2, widen, 0)

        def narrow(step, carry):
            columns = pl.ds(pl.multiple_of(step * 512, 512), 512)
            block[:, columns] = mm(inner_ref[...], down_ref[e, :, columns]).astype(BF16)
            return carry

        lax.fori_loop(0, 4, narrow, 0)

    def region(p, k):
        return () if p == 2 else (k,)

    def slot_of(p, line, k):
        return 64 * p + line * 4 + (0 if p == 2 else k)

    def relay_slot(p, number, k):
        return 64 * p + 32 + number * 4 + (0 if p == 2 else k)

    def send_chunk(k, e):
        for p, (axis, a, b) in enumerate(PARTS):
            columns = pl.ds(BEGIN[p], WIDTH[p])
            every = (slice(None),) * (2 if p == 2 else 1)
            for shift in (k,) if p == 2 else CHUNKS:
                chosen = {2: k} if p == 2 else {axis: shift, 2: k}

                def source(of_core):
                    return view(rows_ref, e, of_core, columns, chosen)

                def target(ref):
                    return ref.at[region(p, k) + every + (slots(e),)]

                line = rows_in[p].at[2 * ((4 - shift) % 4) + core]
                index = slot_of(p, 2 * ((4 - shift) % 4) + core, k)
                if shift == 2:
                    sends.go(source(0), target(from_left[p]), relay_slot(p, 0, k), torus.place(axis, 1))
                    sends.go(source(1), target(from_right[p]), relay_slot(p, 1, k), torus.place(axis, 3))
                elif shift == 0:
                    sends.go(source(1 - core), target(line), index, torus.partner())
                    sends.keep(source(core), target(line), index)
                else:
                    for of_core in range(2):
                        sends.go(source(of_core), target(line), index, torus.place(axis, shift, of_core))

    def pass_on(p, k):
        axis = PARTS[p][0]
        for number, (relay, shift) in enumerate(((from_left[p], 1), (from_right[p], 3))):
            part = relay.at[region(p, k)] if p != 2 else relay
            sends.landed(part, relay_slot(p, number, k))
            sends.go(
                part,
                rows_in[p].at[(4 + core,) + region(p, k)],
                slot_of(p, 4 + core, k),
                torus.place(axis, shift, number),
            )

    def arrived(p, k):
        for line in range(8):
            sends.landed(rows_in[p].at[(line,) + region(p, k)], slot_of(p, line, k))

    before = None
    for k in CHUNKS:
        loads[k].wait()
        expert(k, 0)
        send_chunk(k, 0)
        expert(k, 1)
        if before is not None:
            for p in range(2):
                pass_on(p, before)
            if before == 2:
                pass_on(2, 2)
        send_chunk(k, 1)
        before = k
    for p in range(2):
        pass_on(p, before)

    def add_up(p, second):
        def one(first, carry):
            i, k = ordered(p, second, first)
            rows = rows_in[p][:, i, k].reshape(128, WIDTH[p])
            sums[p][second, first] = mm(mix_ref[p, second * 4 + first], rows).astype(BF16)
            return carry

        lax.fori_loop(0, 4, one, 0, unroll=True)

    def first_sums(p):
        b = PARTS[p][2]
        add_up(p, 2)
        sends.go(sums[p].at[2, 0:2], add_over[p], 64 * p + 42, torus.place(b, 1))
        sends.go(sums[p].at[2, 2:4], add_under[p], 64 * p + 43, torus.place(b, 3))

    arrived(0, 2)
    first_sums(0)
    for p in range(3):
        if p == 2:
            arrived(2, 0)
        else:
            for k in CHUNKS[1:] if p == 0 else CHUNKS:
                arrived(p, k)
        if p > 0:
            first_sums(p)
    for p, (axis, a, b) in enumerate(PARTS):
        add_up(p, 1)
        sends.go(sums[p].at[1, 2:4], over[p].at[2:4], 64 * p + 44, torus.place(b, 1))
        add_up(p, 3)
        sends.go(sums[p].at[3, 0:2], under[p].at[0:2], 64 * p + 45, torus.place(b, 3))
    for p, (axis, a, b) in enumerate(PARTS):
        sends.landed(add_over[p], 64 * p + 42)
        sums[p][1, 0:2] = (sums[p][1, 0:2].astype(F32) + add_over[p][...].astype(F32)).astype(BF16)
        sends.go(sums[p].at[1, 0:2], over[p].at[0:2], 64 * p + 46, torus.place(b, 1))
        sends.landed(add_under[p], 64 * p + 43)
        sums[p][3, 2:4] = (sums[p][3, 2:4].astype(F32) + add_under[p][...].astype(F32)).astype(BF16)
        sends.go(sums[p].at[3, 2:4], under[p].at[2:4], 64 * p + 47, torus.place(b, 3))
    for p in range(3):
        add_up(p, 0)
    low, high = pl.ds(0, 64), pl.ds(64, 64)
    for p, (axis, a, b) in enumerate(PARTS):
        sends.landed(over[p].at[2:4], 64 * p + 44)
        sends.landed(under[p].at[0:2], 64 * p + 45)
        sends.landed(over[p].at[0:2], 64 * p + 46)
        sends.landed(under[p].at[2:4], 64 * p + 47)
        for first in (2, 1, 3, 0):
            total = sums[p][0, first].astype(F32) + over[p][first].astype(F32) + under[p][first].astype(F32)
            sums[p][0, first] = total.astype(BF16)
            if first == 2:
                sends.go(sums[p].at[0, 2, low], over[p].at[4, low], 64 * p + 48, torus.place(a, 1))
                sends.go(sums[p].at[0, 2, high], under[p].at[4, high], 64 * p + 49, torus.place(a, 3))
            elif first == 1:
                sends.go(sums[p].at[0, 1, high], over[p].at[5, high], 64 * p + 50, torus.place(a, 1))
            elif first == 3:
                sends.go(sums[p].at[0, 3, low], under[p].at[5, low], 64 * p + 51, torus.place(a, 3))
    for p, (axis, a, b) in enumerate(PARTS):
        sends.landed(over[p].at[4, low], 64 * p + 48)
        sums[p][0, 1, :64] = (sums[p][0, 1, :64].astype(F32) + over[p][4, :64].astype(F32)).astype(BF16)
        sends.go(sums[p].at[0, 1, low], over[p].at[5, low], 64 * p + 52, torus.place(a, 1))
        sends.landed(under[p].at[4, high], 64 * p + 49)
        sums[p][0, 3, 64:] = (sums[p][0, 3, 64:].astype(F32) + under[p][4, 64:].astype(F32)).astype(BF16)
        sends.go(sums[p].at[0, 3, high], under[p].at[5, high], 64 * p + 53, torus.place(a, 3))
    for p, (axis, a, b) in enumerate(PARTS):
        sends.landed(over[p].at[5, high], 64 * p + 50)
        sends.landed(under[p].at[5, low], 64 * p + 51)
        sends.landed(over[p].at[5, low], 64 * p + 52)
        sends.landed(under[p].at[5, high], 64 * p + 53)
        columns = pl.ds(BEGIN[p], WIDTH[p])
        total = sums[p][0, 0].astype(F32) + over[p][5].astype(F32) + under[p][5].astype(F32)
        out_ref[:, columns] = (hidden_ref[:, columns].astype(F32) + total).astype(BF16)
    sends.finish()


def combine(rows, expert_gate, expert_up, expert_down, mix, hidden):
    vmem = pl.BlockSpec(memory_space=pltpu.VMEM)
    hbm = pl.BlockSpec(memory_space=pl.ANY)
    return pl.pallas_call(
        combine_kernel,
        out_shape=jax.ShapeDtypeStruct(hidden.shape, BF16),
        in_specs=[hbm] * 4 + [vmem] * 2,
        out_specs=vmem,
        scratch_shapes=[
            pltpu.VMEM(rows.shape, BF16),
            pltpu.VMEM((256, expert_gate.shape[2]), BF16),
            pltpu.VMEM(expert_gate.shape, BF16),
            pltpu.VMEM(expert_up.shape, BF16),
            pltpu.VMEM(expert_down.shape, BF16),
            pltpu.SemaphoreType.DMA((4,)),
            pltpu.SemaphoreType.DMA((3, 2)),
        ]
        + [pltpu.VMEM((8, 4, 4, 16, w), BF16) for w in WIDTH]
        + [pltpu.VMEM((4, 4, 16, w), BF16) for w in WIDTH] * 2
        + [pltpu.VMEM((4, 4, 128, w), BF16) for w in WIDTH]
        + [pltpu.VMEM((6, 128, w), BF16) for w in WIDTH] * 2
        + [pltpu.VMEM((2, 128, w), BF16) for w in WIDTH] * 2
        + [pltpu.SemaphoreType.DMA((208,)), pltpu.SemaphoreType.DMA((192,))],
        compiler_params=pltpu.CompilerParams(
            collective_id=2, has_side_effects=True, vmem_limit_bytes=58 * 1024 * 1024
        ),
        cost_estimate=pl.CostEstimate(flops=20_000_000_000, bytes_accessed=10_000_000, transcendentals=0),
    )(rows, expert_gate, expert_up, expert_down, mix, hidden)


def moe(hidden_state, normed, expert_ids, gate_weights, expert_gate, expert_up, expert_down):
    rows, mix = dispatch(normed, expert_ids.T, gate_weights.T)
    return combine(rows, expert_gate, expert_up, expert_down, mix, hidden_state)


def shards(
    residual_in,
    query_input,
    key_input,
    value_input,
    out_gate,
    write_strength,
    decay_rate,
    head_gain,
    out_proj,
    post_gain,
    expert_ids,
    gate_weights,
    expert_gate,
    expert_up,
    expert_down,
):
    stride = lax.axis_size("seq") // 4
    hidden_state, normed = mixer(
        query_input,
        key_input,
        value_input,
        out_gate,
        residual_in,
        out_proj,
        write_strength,
        decay_rate,
        head_gain,
        post_gain,
        stride,
    )
    return moe(hidden_state, normed, expert_ids, gate_weights, expert_gate, expert_up, expert_down)


def solution(mesh):
    both = ("seq", "exp")
    placed = (
        P(both, None),
        P(both, None),
        P(both, None),
        P(both, None),
        P(both, None),
        P(both, None),
        P(both, None),
        P(),
        P(None, "exp"),
        P(),
        P(both, None),
        P(both, None),
        P(both, None, None),
        P(both, None, None),
        P(both, None, None),
    )
    return jax.shard_map(shards, mesh=mesh, in_specs=placed, out_specs=P(both, None), check_vma=False)
```

```python
from functools import partial

import jax
import jax.numpy as jnp
from jax import lax
from jax.experimental import pallas as pl
from jax.experimental.pallas import tpu as pltpu
from jax.sharding import PartitionSpec as P

D = 2048
HK = 8
HV = 16
DK = 128
DV = 128
TOP = 10
TOGETHER = 1
GROUP = 16

F32 = jnp.float32
BF16 = jnp.bfloat16
MESH = pl.DeviceIdType.MESH


def mm(a, b):
    return jnp.dot(a, b, preferred_element_type=F32)


def mm_t(a, b):
    return lax.dot_general(a, b, (((1,), (1,)), ((), ())), preferred_element_type=F32)


def split(x):
    high = x.astype(BF16)
    return high, (x - high.astype(F32)).astype(BF16)


def mm3(a, b):
    return mm(a[0], b[1]) + mm(jnp.concatenate([a[0], a[1]], axis=1), jnp.concatenate([b[0], b[0]], axis=0))


def mm2(a, b):
    return mm(a[0], b) + mm(a[1], b)


def iota(axis):
    return lax.broadcasted_iota(jnp.int32, (128, 128), axis)


def rows_of(row):
    return jnp.broadcast_to(row, (128, 128))


def unit_inverse(lower):
    row, col = iota(0), iota(1)
    eye = jnp.where(row == col, 1.0, 0.0)
    inverse = eye - jnp.where((row >> 1) == (col >> 1), lower, 0.0)
    for level in range(1, 7):
        mask = ((row >> (level + 1)) == (col >> (level + 1))) & ((row >> level) != (col >> level))
        part = split(jnp.where(mask, lower, 0.0))
        blocks = split(inverse)
        inverse = inverse - mm3(blocks, split(mm3(part, blocks)))
    return inverse


def mixer_kernel(
    seq_size,
    exp_size,
    stride,
    q_hbm,
    k_hbm,
    v_hbm,
    gate_hbm,
    residual_hbm,
    proj_hbm,
    rate_ref,
    beta_ref,
    gain_ref,
    post_gain_ref,
    hidden_ref,
    normed_ref,
    q_ref,
    k_ref,
    v_ref,
    gate_ref,
    residual_ref,
    proj,
    core_out,
    logs,
    local_out,
    query_high,
    query_low,
    newest_of,
    key_of,
    maps,
    adds,
    maps_in,
    adds_in,
    prefix,
    prefix_add,
    last_map,
    last_add,
    groups_in,
    groups_add,
    states,
    states_in,
    load,
    send1,
    recv1,
    send2,
    recv2,
    send3,
    recv3,
    proj_send,
    proj_recv,
):
    lines = GROUP // exp_size
    groups = seq_size // lines
    seq, exp = lax.axis_index("seq"), lax.axis_index("exp")
    group = seq // lines
    rank = (seq % lines) * exp_size + exp

    loads = [
        pltpu.make_async_copy(source, target, load.at[number])
        for number, (source, target) in enumerate(
            [
                (k_hbm, k_ref),
                (q_hbm, q_ref),
                (v_hbm, v_ref),
                (gate_hbm, gate_ref),
                (residual_hbm, residual_ref),
                (proj_hbm, proj.at[exp]),
            ]
        )
    ]
    for copy in loads:
        copy.start()

    def device(of_group, of_rank):
        return (of_group * lines + of_rank // exp_size, of_rank % exp_size)

    core = seq % 2
    spot = (seq // stride) % 4

    def ring_seq(shift):
        return seq + ((spot + shift) % 4 - spot) * stride

    def ring_exp(shift):
        return lax.rem(exp + shift, 4)

    partner = (seq + 1 - 2 * core, exp)
    rows = proj_hbm.shape[0] // 8
    half = rows // 2

    def piece(x_shift, spot_shift, begin, size):
        row = pl.multiple_of(core * (4 * rows) + (spot + spot_shift) % 4 * rows + begin, half)
        return proj.at[ring_exp(x_shift), pl.ds(row, size)]

    counter = [0]

    def proj_copy(ref, recv_index, to, source=None):
        number = counter[0]
        counter[0] += 1
        return pltpu.make_async_remote_copy(
            src_ref=ref if source is None else source,
            dst_ref=ref,
            send_sem=proj_send.at[number],
            recv_sem=proj_recv.at[recv_index],
            device_id=to,
            device_id_type=MESH,
        )

    def landing(ref, recv_index):
        return pltpu.make_async_copy(ref, ref, proj_recv.at[recv_index])

    own = proj_hbm.at[pl.ds(pl.multiple_of(core * (4 * rows) + spot * rows, half), rows)]
    mine = piece(0, 0, 0, rows)
    right, left = (seq, ring_exp(1)), (seq, ring_exp(3))
    above, below = (ring_seq(1), exp), (ring_seq(3), exp)
    x_first = [proj_copy(mine, 0, right, own), proj_copy(mine, 1, left, own)]
    x_second = [proj_copy(piece(3, 0, 0, half), 2, right), proj_copy(piece(1, 0, half, half), 3, left)]
    x_landing = [
        landing(piece(3, 0, 0, rows), 0),
        landing(piece(1, 0, 0, rows), 1),
        landing(piece(2, 0, 0, half), 2),
        landing(piece(2, 0, half, half), 3),
    ]
    shifts = (3, 1, 2)
    z_first, z_second, z_landing, across, across_landing = [], [], [], [], []
    for number, shift in enumerate(shifts):
        at = 4 + 4 * number
        z_first.append(
            [proj_copy(piece(shift, 0, 0, rows), at, above), proj_copy(piece(shift, 0, 0, rows), at + 1, below)]
        )
        z_second.append(
            [proj_copy(piece(shift, 3, 0, half), at + 2, above), proj_copy(piece(shift, 1, half, half), at + 3, below)]
        )
        z_landing.append(
            [
                landing(piece(shift, 3, 0, rows), at),
                landing(piece(shift, 1, 0, rows), at + 1),
                landing(piece(shift, 2, 0, half), at + 2),
                landing(piece(shift, 2, half, half), at + 3),
            ]
        )
        across.append([proj_copy(piece(shift, n, 0, rows), 16 + 4 * number + n, partner) for n in range(4)])
        other = (1 - core) * (4 * rows)
        across_landing.append(
            [
                landing(
                    proj.at[
                        ring_exp(shift), pl.ds(pl.multiple_of(other + (spot + n) % 4 * rows, half), rows)
                    ],
                    16 + 4 * number + n,
                )
                for n in range(4)
            ]
        )

    barrier = pltpu.get_barrier_semaphore()

    def greet(to):
        pl.semaphore_signal(barrier, inc=1, device_id=to, device_id_type=MESH)

    def greet_rank(step, carry):
        greet(device(group, lax.rem(rank + step, GROUP)))
        return carry

    def greet_group(step, carry):
        greet(device(lax.rem(group + step, groups), rank))
        return carry

    lax.fori_loop(1, GROUP, greet_rank, 0)
    lax.fori_loop(1, groups, greet_group, 0)
    for to in (right, left, above, below, partner):
        greet(to)
    pl.semaphore_wait(barrier, GROUP - 1 + groups - 1 + 5)

    for copy in x_first:
        copy.start()

    row, col = iota(0), iota(1)
    upto = jnp.where(row <= col, 1.0, 0.0).astype(BF16)
    rate = rate_ref[...]
    first, rest = split(rate)
    last = (rate - first.astype(F32) - rest.astype(F32)).astype(BF16)
    logs[...] = -(mm(first, upto) + (mm(rest, upto) + mm(last, upto)))
    for copy in loads[:3]:
        copy.wait()

    def map_copies(head, to):
        return [
            pltpu.make_async_remote_copy(
                src_ref=source.at[head],
                dst_ref=target.at[to],
                send_sem=send1.at[number, head],
                recv_sem=recv1.at[number, to],
                device_id=device(group, head),
                device_id_type=MESH,
            )
            for number, (source, target) in enumerate([(maps, maps_in), (adds, adds_in)])
        ]

    def map_keeps(head, to):
        return [
            pltpu.make_async_copy(maps.at[head], maps_in.at[to], recv1.at[0, to]),
            pltpu.make_async_copy(adds.at[head], adds_in.at[to], recv1.at[1, to]),
        ]

    def key_head(kh):
        columns = pl.ds(pl.multiple_of(kh * DK, DK), DK)
        k_raw = k_ref[:, columns]
        k_wide = k_raw.astype(F32)
        k_inv = lax.rsqrt(jnp.sum(k_wide * k_wide, axis=1, keepdims=True) + 1e-6)
        k_inv = jnp.broadcast_to(k_inv, (128, 128))
        k_inv_row = k_inv.T
        k_t = k_wide.T.astype(BF16)
        gram = mm_t(k_raw, k_raw) * k_inv * k_inv_row
        for part in range(HV // HK):
            h = kh * (HV // HK) + part
            head_columns = pl.ds(pl.multiple_of(h * DV, DV), DV)
            log_row = rows_of(logs[pl.ds(h, 1), :])
            log_col = log_row.T
            beta_row = rows_of(beta_ref[pl.ds(h, 1), :])
            beta_col = beta_row.T
            ratio = jnp.where(row >= col, jnp.exp(jnp.where(row >= col, log_col - log_row, 0.0)), 0.0)
            inverse = unit_inverse(jnp.where(row > col, ratio * gram, 0.0) * beta_col)
            v_raw = v_ref[:, head_columns]
            weights = split(inverse * beta_row)
            newest = mm2(weights, v_raw)
            weights = split(inverse * (beta_row * jnp.exp(log_row) * k_inv_row))
            key_matrix = mm2(weights, k_raw)
            log_last = jnp.broadcast_to(logs[pl.ds(h, 1), 127:128], (128, 128))
            fade = k_inv * jnp.exp(log_last - log_col)
            side = split(key_matrix * fade)
            moved = mm(k_t, side[0]) + mm(k_t, side[1])
            maps[h] = jnp.where(row == col, jnp.exp(log_last), 0.0) - moved
            side = split(newest * fade)
            adds[h] = (mm(k_t, side[0]) + mm(k_t, side[1])).astype(BF16)
            newest_of[h] = newest
            key_of[h] = key_matrix

    def local_head(kh, carry):
        columns = pl.ds(pl.multiple_of(kh * DK, DK), DK)
        k_raw, q_raw = k_ref[:, columns], q_ref[:, columns]
        k_wide, q_wide = k_raw.astype(F32), q_raw.astype(F32)
        k_inv = lax.rsqrt(jnp.sum(k_wide * k_wide, axis=1, keepdims=True) + 1e-6)
        q_inv = lax.rsqrt(jnp.sum(q_wide * q_wide, axis=1, keepdims=True) + 1e-6) * DK ** (-0.5)
        mixed = mm_t(q_raw, k_raw) * q_inv * jnp.broadcast_to(k_inv, (128, 128)).T
        for part in range(HV // HK):
            h = kh * (HV // HK) + part
            log_row = rows_of(logs[pl.ds(h, 1), :])
            log_col = log_row.T
            ratio = jnp.where(row >= col, jnp.exp(jnp.where(row >= col, log_col - log_row, 0.0)), 0.0)
            mix = split(mixed * ratio)
            local_out[h] = mm3(mix, split(newest_of[h]))
            effective = split(q_wide * q_inv * jnp.exp(log_col) - mm3(mix, split(key_of[h])))
            query_high[h] = effective[0]
            query_low[h] = effective[1]
        return carry

    def key_heads(step, carry):
        for part in range(TOGETHER):
            key_head(step * TOGETHER + part)
        for part in range(TOGETHER * (HV // HK)):
            h = step * (TOGETHER * (HV // HK)) + part

            @pl.when(h != rank)
            def _():
                for copy in map_copies(h, rank):
                    copy.start()

            @pl.when(h == rank)
            def _():
                for copy in map_keeps(h, rank):
                    copy.start()

        @pl.when(step == 1)
        def _():
            for copy in x_landing[:2]:
                copy.wait()
            for copy in x_second + z_first[0] + z_first[1] + [across[0][0], across[1][0]]:
                copy.start()

        @pl.when(step == HK // TOGETHER - 2)
        def _():
            for copy in x_landing[2:]:
                copy.wait()
            for copy in z_first[2] + [across[2][0]]:
                copy.start()

        return carry

    lax.fori_loop(0, HK // TOGETHER, key_heads, 0)

    for number in range(3):
        for copy in z_landing[number][:2]:
            copy.wait()
        for copy in z_second[number] + [across[number][3], across[number][1]]:
            copy.start()

    middle = GROUP // 2
    for start in (0, middle):
        for copy in map_keeps(start, start):
            copy.wait()
        prefix[start] = maps_in[start]
        prefix_add[start] = adds_in[start].astype(F32)

    def chain(step, carry):
        for start in (0, middle):
            index = start + step
            for copy in map_keeps(index, index):
                copy.wait()
        for start in (0, middle):
            index = start + step
            moved = split(maps_in[index])
            prefix[index] = mm3(moved, split(prefix[index - 1]))
            prefix_add[index] = mm3(moved, split(prefix_add[index - 1])) + adds_in[index].astype(F32)
        return carry

    lax.fori_loop(1, middle, chain, 0)
    moved = split(prefix[GROUP - 1])
    last_map[...] = mm3(moved, split(prefix[middle - 1]))
    last_add[...] = (mm3(moved, split(prefix_add[middle - 1])) + prefix_add[GROUP - 1]).astype(BF16)

    def group_copies(to, source):
        return [
            pltpu.make_async_remote_copy(
                src_ref=kept,
                dst_ref=target.at[source],
                send_sem=send2.at[number, to],
                recv_sem=recv2.at[number, source],
                device_id=device(to, rank),
                device_id_type=MESH,
            )
            for number, (kept, target) in enumerate([(last_map, groups_in), (last_add, groups_add)])
        ]

    def send_group(to, carry):
        for copy in group_copies(to, group):
            copy.start()
        return carry

    lax.fori_loop(group + 1, groups, send_group, 0)
    lax.fori_loop(0, HK, local_head, 0)

    for number in range(3):
        for copy in z_landing[number][2:]:
            copy.wait()
        across[number][2].start()

    def enter(source, state):
        for copy in group_copies(group, source):
            copy.wait_recv()
        return mm3(split(groups_in[source]), split(state)) + groups_add[source].astype(F32)

    entering = split(lax.fori_loop(0, group, enter, jnp.zeros((DK, DV), F32)))
    halfway = split(mm3(split(prefix[middle - 1]), entering) + prefix_add[middle - 1])

    def state_copy(to, head):
        return pltpu.make_async_remote_copy(
            src_ref=states.at[to],
            dst_ref=states_in.at[head],
            send_sem=send3.at[to],
            recv_sem=recv3.at[head],
            device_id=device(group, to),
            device_id_type=MESH,
        )

    def state_keep(to, head):
        return pltpu.make_async_copy(states.at[to], states_in.at[head], recv3.at[head])

    def give(to):
        @pl.when(to != rank)
        def _():
            state_copy(to, rank).start()

        @pl.when(to == rank)
        def _():
            state_keep(to, rank).start()

    states[0] = entering[0]
    states[middle] = halfway[0]
    give(0)
    give(middle)

    def spread(step, carry):
        for start, state in ((0, entering), (middle, halfway)):
            index = start + step
            moved = mm3(split(prefix[index - 1]), state) + prefix_add[index - 1]
            states[index] = moved.astype(BF16)
        for start in (0, middle):
            give(start + step)
        return carry

    lax.fori_loop(1, middle, spread, 0)

    gain = gain_ref[...]
    loads[3].wait()

    def finish(h, carry):
        columns = pl.ds(pl.multiple_of(h * DV, DV), DV)
        gate = gate_ref[:, columns].astype(F32)
        scale = gain * (gate / (1.0 + jnp.exp(-gate)))
        state_keep(h, h).wait()
        state = states_in[h]
        out = local_out[h] + (mm(query_high[h], state) + mm(query_low[h], state))
        inv_rms = lax.rsqrt(jnp.sum(out * out, axis=1, keepdims=True) * (1.0 / DV) + 1e-6)
        core_out[:, columns] = (out * inv_rms * scale).astype(BF16)
        return carry

    lax.fori_loop(0, HV, finish, 0, unroll=4)

    loads[4].wait()
    loads[5].wait()
    for number in range(3):
        for copy in across_landing[number]:
            copy.wait()
    width = proj_hbm.shape[1]

    def project(index, square):
        columns = pl.ds(pl.multiple_of(index * width, width), width)
        mixed = mm(core_out[...], proj[index])
        hidden = (residual_ref[:, columns].astype(F32) + mixed).astype(BF16)
        hidden_ref[:, columns] = hidden
        wide = hidden.astype(F32)
        return square + jnp.sum(wide * wide, axis=1, keepdims=True)

    square = lax.fori_loop(0, exp_size, project, jnp.zeros((128, 1), F32))
    inv_rms = lax.rsqrt(square * (1.0 / D) + 1e-6)
    normed_ref[...] = (hidden_ref[...].astype(F32) * inv_rms * post_gain_ref[...]).astype(BF16)

    def drain(index, carry):
        @pl.when(index != rank)
        def _():
            for copy in map_copies(index, rank):
                copy.wait_send()
            state_copy(index, rank).wait_send()

        return carry

    lax.fori_loop(0, GROUP, drain, 0)

    def drain_group(to, carry):
        for copy in group_copies(to, group):
            copy.wait_send()
        return carry

    lax.fori_loop(group + 1, groups, drain_group, 0)
    for copy in x_first + x_second:
        copy.wait_send()
    for number in range(3):
        for copy in z_first[number] + z_second[number] + across[number]:
            copy.wait_send()


def mixer(query, key, value, gate, residual, proj, strength, rate, head_gain, post_gain, stride):
    seq_size, exp_size = lax.axis_size("seq"), lax.axis_size("exp")
    groups = seq_size * exp_size // GROUP
    tokens = query.shape[0]
    vmem = pl.BlockSpec(memory_space=pltpu.VMEM)
    hbm = pl.BlockSpec(memory_space=pl.ANY)
    square = (128, 128)
    return pl.pallas_call(
        partial(mixer_kernel, seq_size, exp_size, stride),
        out_shape=[jax.ShapeDtypeStruct((tokens, D), BF16)] * 2,
        in_specs=[hbm] * 6 + [vmem] * 4,
        out_specs=[vmem, vmem],
        scratch_shapes=[
            pltpu.VMEM(query.shape, BF16),
            pltpu.VMEM(key.shape, BF16),
            pltpu.VMEM(value.shape, BF16),
            pltpu.VMEM(gate.shape, BF16),
            pltpu.VMEM(residual.shape, BF16),
            pltpu.VMEM((exp_size,) + proj.shape, BF16),
            pltpu.VMEM(value.shape, BF16),
            pltpu.VMEM((HV, tokens), F32),
            pltpu.VMEM((HV,) + square, F32),
            pltpu.VMEM((HV,) + square, BF16),
            pltpu.VMEM((HV,) + square, BF16),
            pltpu.VMEM((HV,) + square, F32),
            pltpu.VMEM((HV,) + square, F32),
            pltpu.VMEM((HV,) + square, F32),
            pltpu.VMEM((HV,) + square, BF16),
            pltpu.VMEM((GROUP,) + square, F32),
            pltpu.VMEM((GROUP,) + square, BF16),
            pltpu.VMEM((GROUP,) + square, F32),
            pltpu.VMEM((GROUP,) + square, F32),
            pltpu.VMEM(square, F32),
            pltpu.VMEM(square, BF16),
            pltpu.VMEM((groups,) + square, F32),
            pltpu.VMEM((groups,) + square, BF16),
            pltpu.VMEM((GROUP,) + square, BF16),
            pltpu.VMEM((HV,) + square, BF16),
            pltpu.SemaphoreType.DMA((6,)),
            pltpu.SemaphoreType.DMA((2, HV)),
            pltpu.SemaphoreType.DMA((2, GROUP)),
            pltpu.SemaphoreType.DMA((2, groups)),
            pltpu.SemaphoreType.DMA((2, groups)),
            pltpu.SemaphoreType.DMA((GROUP,)),
            pltpu.SemaphoreType.DMA((HV,)),
            pltpu.SemaphoreType.DMA((28,)),
            pltpu.SemaphoreType.DMA((28,)),
        ],
        compiler_params=pltpu.CompilerParams(
            collective_id=0, has_side_effects=True, vmem_limit_bytes=56 * 1024 * 1024
        ),
        cost_estimate=pl.CostEstimate(flops=8_000_000_000, bytes_accessed=4_000_000, transcendentals=0),
    )(
        query,
        key,
        value,
        gate,
        residual,
        proj,
        rate.T,
        strength.T,
        head_gain.reshape(1, DV),
        post_gain.reshape(1, D),
    )


PARTS = ((0, 1, 2), (1, 2, 0), (2, 0, 1))
BEGIN = (0, 640, 1280)
WIDTH = (640, 640, 768)
EXTRA = 8
BLOCK = 128 + EXTRA


class Torus:
    def __init__(self):
        seq, self.exp = lax.axis_index("seq"), lax.axis_index("exp")
        self.core = seq % 2
        self.at = (self.exp, (seq // 2) % 4, seq // 8)

    def place(self, axis, shift, core=None):
        x, y, z = [(c + shift) % 4 if n == axis else c for n, c in enumerate(self.at)]
        return ((z * 4 + y) * 2 + (self.core if core is None else core), x)

    def partner(self):
        return self.place(0, 0, 1 - self.core)

    def greet(self):
        barrier = pltpu.get_barrier_semaphore()
        others = [self.partner()]
        for axis in range(3):
            for shift in (1, 3):
                others += [self.place(axis, shift), self.place(axis, shift, 1 - self.core)]
        for to in others:
            pl.semaphore_signal(barrier, inc=1, device_id=to, device_id_type=MESH)
        pl.semaphore_wait(barrier, len(others))


class Sends:
    def __init__(self, send, recv):
        self.send, self.recv, self.count, self.open = send, recv, 0, []

    def go(self, source, target, index, to):
        copy = pltpu.make_async_remote_copy(
            src_ref=source,
            dst_ref=target,
            send_sem=self.send.at[self.count],
            recv_sem=self.recv.at[index],
            device_id=to,
            device_id_type=MESH,
        )
        self.count += 1
        copy.start()
        self.open.append(copy)

    def keep(self, source, target, index):
        pltpu.make_async_copy(source, target, self.recv.at[index]).start()

    def landed(self, target, index):
        pltpu.make_async_copy(target, target, self.recv.at[index]).wait()

    def finish(self):
        for copy in self.open:
            copy.wait_send()


def view(ref, expert, core, columns, chosen):
    x, y, z = [chosen.get(axis, slice(None)) for axis in range(3)]
    return ref.at[z, expert, x, y, core, slice(None), columns]


def ordered(part, second, first):
    return (second, first) if part == 0 else (first, second)


def slots(expert):
    return pl.ds(8 * expert, 8)


def dispatch_kernel(normed_ref, ids_ref, weight_ref, out_ref, mix_ref, extra, *scratch):
    blocks, rows_out = scratch[0:3], scratch[3:6]
    from_left, from_right = scratch[6:9], scratch[9:12]
    sends = Sends(scratch[12], scratch[13])
    torus = Torus()
    extra[...] = jnp.full(extra.shape, -1.0, F32)
    extra[0, :TOP] = ids_ref[...].astype(F32)
    extra[1, :TOP] = weight_ref[...]
    for p in range(3):
        columns = pl.ds(BEGIN[p], WIDTH[p])
        blocks[p][0, 0, :128, :] = normed_ref[:, columns]
        for number in range(4):
            lanes = slice(128 * number, 128 * (number + 1))
            rows = slice(8 * (number % 2), 8 * (number % 2) + 8)
            blocks[p][0, 0, 128:, lanes] = extra[number // 2, rows].astype(BF16)
        blocks[p][0, 0, 128:, 512:] = jnp.zeros((EXTRA, WIDTH[p] - 512), BF16)
    torus.greet()
    low, high = pl.ds(0, 72), pl.ds(72, BLOCK - 72)

    def hand_on(p, first):
        b = PARTS[p][2]
        block = blocks[p].at[0, first]
        sends.go(block, blocks[p].at[3, first], 64 * p + 4 + first, torus.place(b, 1))
        sends.go(block, blocks[p].at[1, first], 64 * p + 8 + first, torus.place(b, 3))

    def gathered(p, second, first):
        sends.landed(blocks[p].at[second, first], 64 * p + (4 if second == 3 else 8) + first)

    for p, (_, a, b) in enumerate(PARTS):
        own = blocks[p].at[0, 0]
        sends.go(own, blocks[p].at[0, 3], 64 * p + 0, torus.place(a, 1))
        sends.go(own, blocks[p].at[0, 1], 64 * p + 1, torus.place(a, 3))
    for p in range(3):
        hand_on(p, 0)
    for p, (_, a, b) in enumerate(PARTS):
        sends.landed(blocks[p].at[0, 3], 64 * p + 0)
        sends.go(blocks[p].at[0, 3, low], blocks[p].at[0, 2, low], 64 * p + 2, torus.place(a, 1))
        sends.landed(blocks[p].at[0, 1], 64 * p + 1)
        sends.go(blocks[p].at[0, 1, high], blocks[p].at[0, 2, high], 64 * p + 3, torus.place(a, 3))
        hand_on(p, 1)
        hand_on(p, 3)
    for p in range(3):
        sends.landed(blocks[p].at[0, 2, low], 64 * p + 2)
        sends.landed(blocks[p].at[0, 2, high], 64 * p + 3)
        hand_on(p, 2)

    row, col = iota(0), iota(1)
    earlier = jnp.where(row < col, 1.0, 0.0).astype(BF16)
    spread_row = lax.broadcasted_iota(jnp.int32, (128, 16), 0)
    spread_col = lax.broadcasted_iota(jnp.int32, (128, 16), 1)
    spread = jnp.where((spread_row >> 3) == spread_col, 1.0, 0.0).astype(BF16)
    slot = (row & 7).astype(F32)
    line = lax.broadcasted_iota(jnp.int32, (16, 128), 0)

    def extract(p, second):
        place = [(c + (line >> 2)) & 3 if n == PARTS[p][0] else c for n, c in enumerate(torus.at)]
        device = ((place[2] * 4 + place[1]) * 2 + ((line >> 1) & 1)) * 4 + place[0]
        expert = (device * 2 + (line & 1)).astype(F32)

        def one(first, carry):
            block = blocks[p].at[second, first]
            extras = [block[128:, 128 * n : 128 * (n + 1)].astype(F32) for n in range(4)]
            named = jnp.zeros((16, 128), F32)
            weight = jnp.zeros((16, 128), F32)
            for choice in range(TOP):
                number, at = choice // 8, slice(choice % 8, choice % 8 + 1)
                hit = expert == jnp.broadcast_to(extras[number][at, :], (16, 128))
                named = jnp.where(hit, 1.0, named)
                weight = jnp.where(hit, jnp.broadcast_to(extras[2 + number][at, :], (16, 128)), weight)
            before = mm(named.astype(BF16), earlier)
            code = jnp.where(named > 0.5, before, -1.0).astype(BF16)
            here = mm(spread, code) == slot
            pick = jnp.where(here, 1.0, 0.0).astype(BF16)
            mix = jnp.where(here, mm(spread, weight.astype(BF16)), 0.0)
            mix_ref[p, second * 4 + first] = mix.T.astype(BF16)
            taken = mm(pick, block[:128, :]).astype(BF16).reshape(8, 16, WIDTH[p])
            i, k = ordered(p, second, first)
            rows_out[p][:, i, k] = taken
            return carry

        lax.fori_loop(0, 4, one, 0, unroll=True)

    core = torus.core

    def chunk(p, second):
        return (second,) if p == 0 else (slice(None), second)

    def slot_of(p, place, of_core, second):
        return 64 * p + 24 + place * 8 + of_core * 4 + second

    def columns_of(p):
        return pl.ds(BEGIN[p], WIDTH[p])

    def every(p):
        return (slice(None),) if p == 0 else ()

    def send_chunk(p, second):
        axis, _, b = PARTS[p]
        rows = rows_out[p]
        for number, (relay, shift) in enumerate(((from_left[p], 1), (from_right[p], 3))):
            sends.go(
                rows.at[(4 + number,) + chunk(p, second)],
                relay.at[chunk(p, second)],
                64 * p + 14 + number * 4 + second,
                torus.place(axis, shift),
            )
        for e in range(2):

            def source(line):
                return rows.at[(line,) + chunk(p, second) + every(p) + (slots(e),)]

            for shift in (1, 3):
                for to_core in range(2):
                    sends.go(
                        source(2 * shift + to_core),
                        view(out_ref, e, core, columns_of(p), {axis: 4 - shift, b: second}),
                        slot_of(p, 4 - shift, core, second),
                        torus.place(axis, shift, to_core),
                    )
            here = view(out_ref, e, core, columns_of(p), {axis: 0, b: second})
            sends.go(source(1 - core), here, slot_of(p, 0, core, second), torus.partner())
            sends.keep(source(core), here, slot_of(p, 0, core, second))

    def pass_on(p, second):
        axis, _, b = PARTS[p]
        for number, (relay, shift) in enumerate(((from_left[p], 1), (from_right[p], 3))):
            sends.landed(relay.at[chunk(p, second)], 64 * p + 14 + number * 4 + second)
            for e in range(2):
                sends.go(
                    relay.at[chunk(p, second) + every(p) + (slots(e),)],
                    view(out_ref, e, core, columns_of(p), {axis: 2, b: second}),
                    slot_of(p, 2, core, second),
                    torus.place(axis, shift, number),
                )

    for p in range(3):
        extract(p, 0)
        send_chunk(p, 0)
    for p, (_, a, b) in enumerate(PARTS):
        gathered(p, 3, 0)
        gathered(p, 3, 1)
        sends.go(blocks[p].at[3, 0:2], blocks[p].at[2, 0:2], 64 * p + 12, torus.place(b, 1))
        gathered(p, 1, 3)
        gathered(p, 1, 2)
        sends.go(blocks[p].at[1, 2:4], blocks[p].at[2, 2:4], 64 * p + 13, torus.place(b, 3))
    for p in range(3):
        gathered(p, 3, 3)
        gathered(p, 3, 2)
        extract(p, 3)
        send_chunk(p, 3)
    for p in range(3):
        gathered(p, 1, 0)
        gathered(p, 1, 1)
        extract(p, 1)
        send_chunk(p, 1)
        pass_on(p, 0)
    for p in range(3):
        sends.landed(blocks[p].at[2, 0:2], 64 * p + 12)
        sends.landed(blocks[p].at[2, 2:4], 64 * p + 13)
        extract(p, 2)
        send_chunk(p, 2)
        pass_on(p, 3)
    for second in (1, 2):
        for p in range(3):
            pass_on(p, second)
    both = slice(None)
    for p, (axis, a, b) in enumerate(PARTS):
        for place in range(4):
            for of_core in range(2):
                for second in range(4):
                    sends.landed(
                        view(out_ref, both, of_core, columns_of(p), {axis: place, b: second}),
                        slot_of(p, place, of_core, second),
                    )
    sends.finish()


def dispatch(normed, ids, weights):
    vmem = pl.BlockSpec(memory_space=pltpu.VMEM)
    hbm = pl.BlockSpec(memory_space=pl.ANY)
    return pl.pallas_call(
        dispatch_kernel,
        out_shape=[
            jax.ShapeDtypeStruct((4, 2, 4, 4, 2, 8, D), BF16),
            jax.ShapeDtypeStruct((3, 16, 128, 128), BF16),
        ],
        in_specs=[vmem] * 3,
        out_specs=[hbm, vmem],
        scratch_shapes=[pltpu.VMEM((2, 16, 128), F32)]
        + [pltpu.VMEM((4, 4, BLOCK, w), BF16) for w in WIDTH]
        + [pltpu.VMEM((8, 4, 4, 16, w), BF16) for w in WIDTH]
        + [pltpu.VMEM((4, 4, 16, w), BF16) for w in WIDTH] * 2
        + [pltpu.SemaphoreType.DMA((240,)), pltpu.SemaphoreType.DMA((192,))],
        compiler_params=pltpu.CompilerParams(
            collective_id=1, has_side_effects=True, vmem_limit_bytes=58 * 1024 * 1024
        ),
        cost_estimate=pl.CostEstimate(flops=2_000_000_000, bytes_accessed=10_000_000, transcendentals=0),
    )(normed, ids, weights)


CHUNKS = (2, 1, 3, 0)


def combine_kernel(
    rows_hbm,
    gate_hbm,
    up_hbm,
    down_hbm,
    mix_ref,
    hidden_ref,
    out_ref,
    rows_ref,
    inner_ref,
    gate_ref,
    up_ref,
    down_ref,
    load,
    fetch,
    *scratch,
):
    rows_in, from_left, from_right = scratch[0:3], scratch[3:6], scratch[6:9]
    sums, over, under, add_over, add_under = (
        scratch[9:12],
        scratch[12:15],
        scratch[15:18],
        scratch[18:21],
        scratch[21:24],
    )
    sends = Sends(scratch[24], scratch[25])
    torus = Torus()
    core = torus.core
    loads = [pltpu.make_async_copy(rows_hbm.at[k], rows_ref.at[k], load.at[k]) for k in range(4)]
    weights = [
        [
            pltpu.make_async_copy(source.at[e], target.at[e], fetch.at[number, e])
            for number, (source, target) in enumerate(((gate_hbm, gate_ref), (up_hbm, up_ref), (down_hbm, down_ref)))
        ]
        for e in range(2)
    ]
    loads[CHUNKS[0]].start()
    for copy in weights[0] + weights[1]:
        copy.start()
    for k in CHUNKS[1:]:
        loads[k].start()
    torus.greet()

    def expert(k, e):
        if k == CHUNKS[0]:
            for copy in weights[e]:
                copy.wait()
        block = rows_ref.at[k, e].reshape(256, D)

        def widen(step, carry):
            columns = pl.ds(pl.multiple_of(step * 256, 256), 256)
            gate_part = mm(block[...], gate_ref[e, :, columns])
            up_part = mm(block[...], up_ref[e, :, columns])
            inner_ref[:, columns] = (gate_part / (1.0 + jnp.exp(-gate_part)) * up_part).astype(BF16)
            return carry

        lax.fori_loop(0, 2, widen, 0)

        def narrow(step, carry):
            columns = pl.ds(pl.multiple_of(step * 512, 512), 512)
            block[:, columns] = mm(inner_ref[...], down_ref[e, :, columns]).astype(BF16)
            return carry

        lax.fori_loop(0, 4, narrow, 0)

    def region(p, k):
        return () if p == 2 else (k,)

    def slot_of(p, line, k):
        return 64 * p + line * 4 + (0 if p == 2 else k)

    def relay_slot(p, number, k):
        return 64 * p + 32 + number * 4 + (0 if p == 2 else k)

    def send_chunk(k, e):
        for p, (axis, a, b) in enumerate(PARTS):
            columns = pl.ds(BEGIN[p], WIDTH[p])
            every = (slice(None),) * (2 if p == 2 else 1)
            for shift in (k,) if p == 2 else CHUNKS:
                chosen = {2: k} if p == 2 else {axis: shift, 2: k}

                def source(of_core):
                    return view(rows_ref, e, of_core, columns, chosen)

                def target(ref):
                    return ref.at[region(p, k) + every + (slots(e),)]

                line = rows_in[p].at[2 * ((4 - shift) % 4) + core]
                index = slot_of(p, 2 * ((4 - shift) % 4) + core, k)
                if shift == 2:
                    sends.go(source(0), target(from_left[p]), relay_slot(p, 0, k), torus.place(axis, 1))
                    sends.go(source(1), target(from_right[p]), relay_slot(p, 1, k), torus.place(axis, 3))
                elif shift == 0:
                    sends.go(source(1 - core), target(line), index, torus.partner())
                    sends.keep(source(core), target(line), index)
                else:
                    for of_core in range(2):
                        sends.go(source(of_core), target(line), index, torus.place(axis, shift, of_core))

    def pass_on(p, k):
        axis = PARTS[p][0]
        for number, (relay, shift) in enumerate(((from_left[p], 1), (from_right[p], 3))):
            part = relay.at[region(p, k)] if p != 2 else relay
            sends.landed(part, relay_slot(p, number, k))
            sends.go(
                part,
                rows_in[p].at[(4 + core,) + region(p, k)],
                slot_of(p, 4 + core, k),
                torus.place(axis, shift, number),
            )

    def arrived(p, k):
        for line in range(8):
            sends.landed(rows_in[p].at[(line,) + region(p, k)], slot_of(p, line, k))

    before = None
    for k in CHUNKS:
        loads[k].wait()
        expert(k, 0)
        send_chunk(k, 0)
        expert(k, 1)
        if before is not None:
            for p in range(2):
                pass_on(p, before)
            if before == 2:
                pass_on(2, 2)
        send_chunk(k, 1)
        before = k
    for p in range(2):
        pass_on(p, before)

    def add_up(p, second):
        def one(first, carry):
            i, k = ordered(p, second, first)
            rows = rows_in[p][:, i, k].reshape(128, WIDTH[p])
            sums[p][second, first] = mm(mix_ref[p, second * 4 + first], rows).astype(BF16)
            return carry

        lax.fori_loop(0, 4, one, 0, unroll=True)

    def first_sums(p):
        b = PARTS[p][2]
        add_up(p, 2)
        sends.go(sums[p].at[2, 0:2], add_over[p], 64 * p + 42, torus.place(b, 1))
        sends.go(sums[p].at[2, 2:4], add_under[p], 64 * p + 43, torus.place(b, 3))

    arrived(0, 2)
    first_sums(0)
    for p in range(3):
        if p == 2:
            arrived(2, 0)
        else:
            for k in CHUNKS[1:] if p == 0 else CHUNKS:
                arrived(p, k)
        if p > 0:
            first_sums(p)
    for p, (axis, a, b) in enumerate(PARTS):
        add_up(p, 1)
        sends.go(sums[p].at[1, 2:4], over[p].at[2:4], 64 * p + 44, torus.place(b, 1))
        add_up(p, 3)
        sends.go(sums[p].at[3, 0:2], under[p].at[0:2], 64 * p + 45, torus.place(b, 3))
    for p, (axis, a, b) in enumerate(PARTS):
        sends.landed(add_over[p], 64 * p + 42)
        sums[p][1, 0:2] = (sums[p][1, 0:2].astype(F32) + add_over[p][...].astype(F32)).astype(BF16)
        sends.go(sums[p].at[1, 0:2], over[p].at[0:2], 64 * p + 46, torus.place(b, 1))
        sends.landed(add_under[p], 64 * p + 43)
        sums[p][3, 2:4] = (sums[p][3, 2:4].astype(F32) + add_under[p][...].astype(F32)).astype(BF16)
        sends.go(sums[p].at[3, 2:4], under[p].at[2:4], 64 * p + 47, torus.place(b, 3))
    for p in range(3):
        add_up(p, 0)
    low, high = pl.ds(0, 64), pl.ds(64, 64)
    for p, (axis, a, b) in enumerate(PARTS):
        sends.landed(over[p].at[2:4], 64 * p + 44)
        sends.landed(under[p].at[0:2], 64 * p + 45)
        sends.landed(over[p].at[0:2], 64 * p + 46)
        sends.landed(under[p].at[2:4], 64 * p + 47)
        for first in (2, 1, 3, 0):
            total = sums[p][0, first].astype(F32) + over[p][first].astype(F32) + under[p][first].astype(F32)
            sums[p][0, first] = total.astype(BF16)
            if first == 2:
                sends.go(sums[p].at[0, 2, low], over[p].at[4, low], 64 * p + 48, torus.place(a, 1))
                sends.go(sums[p].at[0, 2, high], under[p].at[4, high], 64 * p + 49, torus.place(a, 3))
            elif first == 1:
                sends.go(sums[p].at[0, 1, high], over[p].at[5, high], 64 * p + 50, torus.place(a, 1))
            elif first == 3:
                sends.go(sums[p].at[0, 3, low], under[p].at[5, low], 64 * p + 51, torus.place(a, 3))
    for p, (axis, a, b) in enumerate(PARTS):
        sends.landed(over[p].at[4, low], 64 * p + 48)
        sums[p][0, 1, :64] = (sums[p][0, 1, :64].astype(F32) + over[p][4, :64].astype(F32)).astype(BF16)
        sends.go(sums[p].at[0, 1, low], over[p].at[5, low], 64 * p + 52, torus.place(a, 1))
        sends.landed(under[p].at[4, high], 64 * p + 49)
        sums[p][0, 3, 64:] = (sums[p][0, 3, 64:].astype(F32) + under[p][4, 64:].astype(F32)).astype(BF16)
        sends.go(sums[p].at[0, 3, high], under[p].at[5, high], 64 * p + 53, torus.place(a, 3))
    for p, (axis, a, b) in enumerate(PARTS):
        sends.landed(over[p].at[5, high], 64 * p + 50)
        sends.landed(under[p].at[5, low], 64 * p + 51)
        sends.landed(over[p].at[5, low], 64 * p + 52)
        sends.landed(under[p].at[5, high], 64 * p + 53)
        columns = pl.ds(BEGIN[p], WIDTH[p])
        total = sums[p][0, 0].astype(F32) + over[p][5].astype(F32) + under[p][5].astype(F32)
        out_ref[:, columns] = (hidden_ref[:, columns].astype(F32) + total).astype(BF16)
    sends.finish()


def combine(rows, expert_gate, expert_up, expert_down, mix, hidden):
    vmem = pl.BlockSpec(memory_space=pltpu.VMEM)
    hbm = pl.BlockSpec(memory_space=pl.ANY)
    return pl.pallas_call(
        combine_kernel,
        out_shape=jax.ShapeDtypeStruct(hidden.shape, BF16),
        in_specs=[hbm] * 4 + [vmem] * 2,
        out_specs=vmem,
        scratch_shapes=[
            pltpu.VMEM(rows.shape, BF16),
            pltpu.VMEM((256, expert_gate.shape[2]), BF16),
            pltpu.VMEM(expert_gate.shape, BF16),
            pltpu.VMEM(expert_up.shape, BF16),
            pltpu.VMEM(expert_down.shape, BF16),
            pltpu.SemaphoreType.DMA((4,)),
            pltpu.SemaphoreType.DMA((3, 2)),
        ]
        + [pltpu.VMEM((8, 4, 4, 16, w), BF16) for w in WIDTH]
        + [pltpu.VMEM((4, 4, 16, w), BF16) for w in WIDTH] * 2
        + [pltpu.VMEM((4, 4, 128, w), BF16) for w in WIDTH]
        + [pltpu.VMEM((6, 128, w), BF16) for w in WIDTH] * 2
        + [pltpu.VMEM((2, 128, w), BF16) for w in WIDTH] * 2
        + [pltpu.SemaphoreType.DMA((208,)), pltpu.SemaphoreType.DMA((192,))],
        compiler_params=pltpu.CompilerParams(
            collective_id=2, has_side_effects=True, vmem_limit_bytes=58 * 1024 * 1024
        ),
        cost_estimate=pl.CostEstimate(flops=20_000_000_000, bytes_accessed=10_000_000, transcendentals=0),
    )(rows, expert_gate, expert_up, expert_down, mix, hidden)


def moe(hidden_state, normed, expert_ids, gate_weights, expert_gate, expert_up, expert_down):
    rows, mix = dispatch(normed, expert_ids.T, gate_weights.T)
    return combine(rows, expert_gate, expert_up, expert_down, mix, hidden_state)


def shards(
    residual_in,
    query_input,
    key_input,
    value_input,
    out_gate,
    write_strength,
    decay_rate,
    head_gain,
    out_proj,
    post_gain,
    expert_ids,
    gate_weights,
    expert_gate,
    expert_up,
    expert_down,
):
    stride = lax.axis_size("seq") // 4
    hidden_state, normed = mixer(
        query_input,
        key_input,
        value_input,
        out_gate,
        residual_in,
        out_proj,
        write_strength,
        decay_rate,
        head_gain,
        post_gain,
        stride,
    )
    return moe(hidden_state, normed, expert_ids, gate_weights, expert_gate, expert_up, expert_down)


def solution(mesh):
    both = ("seq", "exp")
    placed = (
        P(both, None),
        P(both, None),
        P(both, None),
        P(both, None),
        P(both, None),
        P(both, None),
        P(both, None),
        P(),
        P(None, "exp"),
        P(),
        P(both, None),
        P(both, None),
        P(both, None, None),
        P(both, None, None),
        P(both, None, None),
    )
    return jax.shard_map(shards, mesh=mesh, in_specs=placed, out_specs=P(both, None), check_vma=False)
```
